32 devices in a mesh: groups: 2 (over y), visit: 4 (over z), strip: 2 (over x), band: 2 (over core).
Axes of the slice: x: 2, y: 2, z: 4, core: 2. Of those that a mesh axis runs over, the one named last changes fastest.
Arguments:
- images: bfloat16 [2, 128, 128, 256], P('band', ('groups', 'visit'), 'strip'), parts along dimension 1, may hold values from -8 to 8
- mask_bits: int32 [2, 128, 128, 256], P('band', ('groups', 'visit'), 'strip'), parts along dimension 1, may hold values from 0 to 15
- visit_weight: bfloat16 [2, 128], P('band', ('groups', 'visit')), parts along dimension 1, may hold values from 1 to 4
- intersection: int32 [128, 1], P(('groups', 'visit')), parts along dimension 0, may hold values from 0 to 3, as said below
- patch_owner: int32 [8], P('groups'), parts along dimension 0, may hold values from 0 to 3, each once
Outputs:
- coadd_image: bfloat16 [2, 8, 128, 256], P('band', ('groups', 'visit'), 'strip'), parts along dimension 1
- difference: bfloat16 [2, 128, 128, 256], P('band', ('groups', 'visit'), 'strip'), parts along dimension 1
The draws below stay inside these ranges and needn't reach their ends.
There are 2 independent parts, one for each index of `groups`. The reference program is written for one: setup_inputs(seed, part) draws one part's arguments, and reference() takes and returns one part's arrays. A program takes and returns all parts, laid end to end along the dimension named above; each array names one. Nothing has to cross between parts.
Inputs may be any that keep to these rules, and one draw needn't show every extreme that they name: `intersection`: row j names the patch that piece j intersections. The 16 pieces of one visit index intersect 16 // 8 distinct patches, exactly 8 pieces each; one patch is intersected by 8 pieces of every visit index, and every patch is intersected by some piece. `patch_owner`: A permutation of the patches.
All inputs are finite; a program needn't handle non-finite values.
Results may differ from the reference program's by a relative error of at most 0.0071.
Values may be sent and summed in bfloat16 or wider, within the bound.
A program may use at most 64 MiB of HBM per device.

```python
import math
import jax
import jax.numpy as jnp
from jax import lax

COLS = 256
PIECES_DEV = 16
CAP = 8
BASES = 6
HALF = 9
PATCHES = 4
PIECES = 64
ROWS = 128
BANDS = 2


basis_rows = (0, 0, 1, 0, 2, 1)


basis_cols = (0, 1, 0, 2, 0, 1)


def tap_rows():
    offsets = jnp.arange(2 * HALF + 1).astype(jnp.float32) - HALF
    gaussian = jnp.exp(-offsets * offsets / 18.0)
    centre = jnp.sum(offsets * offsets * gaussian * gaussian) / jnp.sum(gaussian * gaussian)
    tap_table = jnp.stack([gaussian, offsets * gaussian, (offsets * offsets - centre) * gaussian])
    return tap_table / jnp.sqrt(jnp.sum(tap_table * tap_table, axis=1, keepdims=True))


def intersection_table(key):
    base_key = jax.random.fold_in(key, 7001)
    ranking_key, turn_key, order_key = jax.random.split(base_key, 3)
    ranking = jax.random.permutation(ranking_key, PATCHES).astype(jnp.int32)
    rotate = jax.random.randint(turn_key, (), 0, PATCHES - 1).astype(jnp.int32)
    position = jnp.arange(PIECES).astype(jnp.int32)
    visit_index = position // PIECES_DEV
    local_index = position % PIECES_DEV
    group = local_index // CAP
    rank_index = jnp.where(group == 0, 0, 1 + (rotate + visit_index + group - 1) % (PATCHES - 1))
    ordered = ranking[rank_index]

    def shuffle_block(block_key):
        return jax.random.permutation(block_key, PIECES_DEV).astype(jnp.int32)
    shuffles = jax.vmap(shuffle_block)(jax.random.split(order_key, PATCHES))
    chosen = (jnp.arange(PATCHES).astype(jnp.int32)[:, None] * PIECES_DEV + shuffles).reshape(PIECES)
    return ordered[chosen].astype(jnp.int32)


def draw_intersection(key, part):
    return intersection_table(key)[:, None]


def draw_images(key, part):
    patch_ids = intersection_table(key)
    base_key = jax.random.fold_in(key, 7103)
    sky_key, mixing_key, noise_key, scale_key = jax.random.split(base_key, 4)
    sky_field = jax.random.normal(sky_key, (BANDS, PATCHES, ROWS, COLS), jnp.float32)
    taps = tap_rows()
    padded = jnp.pad(sky_field, ((0, 0), (0, 0), (HALF, HALF), (0, 0)))
    vertical = jnp.zeros((3, BANDS, PATCHES, ROWS, COLS), jnp.float32)
    for offset_index in range(2 * HALF + 1):
        vertical = vertical + taps[:, offset_index, None, None, None, None] * padded[None, :, :, offset_index:offset_index + ROWS]
    widened = jnp.pad(vertical, ((0, 0), (0, 0), (0, 0), (0, 0), (HALF, HALF)))
    plane_list = []
    for basis_index in range(BASES):
        total = jnp.zeros((BANDS, PATCHES, ROWS, COLS), jnp.float32)
        for offset_index in range(2 * HALF + 1):
            total = total + taps[basis_cols[basis_index], offset_index] * widened[basis_rows[basis_index], :, :, :, offset_index:offset_index + COLS]
        plane_list.append(total)
    planes = jnp.stack(plane_list)
    mixing = 0.5 * jax.random.normal(mixing_key, (PIECES, BASES), jnp.float32)

    def one_piece(piece_index):
        patch = patch_ids[piece_index]
        sky_plane = lax.dynamic_index_in_dim(sky_field, patch, 1, keepdims=False)
        convolved = lax.dynamic_index_in_dim(planes, patch, 2, keepdims=False)
        piece_key = jax.random.fold_in(noise_key, piece_index)
        noise = 0.3 * jax.random.normal(piece_key, (BANDS, ROWS, COLS), jnp.float32)
        mixed = jnp.sum(mixing[piece_index][:, None, None, None] * convolved, axis=0)
        return sky_plane + mixed + noise
    pieces_all = lax.map(one_piece, jnp.arange(PIECES).astype(jnp.int32))
    result = jnp.clip(jnp.transpose(pieces_all, (1, 0, 2, 3)), -8.0, 8.0)
    return result.astype(jnp.bfloat16)


def set_ends(entries, key, smallest, high):
    extent = entries.shape
    spot = [jax.random.randint(jax.random.fold_in(key, axis), (), 0, extent[axis]) for axis in range(len(extent))]
    entries = entries.at[tuple(spot)].set(smallest)
    longest = extent.index(max(extent))
    spot[longest] = (spot[longest] + 1) % extent[longest]
    return entries.at[tuple(spot)].set(high)


def block_scale(key, dims, shards, smallest, top_value):
    def one(dim, blocks):
        draws = jax.random.uniform(jax.random.fold_in(jax.random.fold_in(key, 6), dim), (blocks,), jnp.float32, smallest / len(shards), top_value / len(shards))
        return jnp.repeat(jnp.exp(draws), dims[dim] // blocks).reshape((-1,) + (1,) * (len(dims) - dim - 1))

    loudness = one(*shards[0])
    for cut in shards[1:]:
        loudness = loudness * one(*cut)
    return loudness


def setup_inputs(seed: int = 0, part: int = 0) -> dict:
    arg_keys = jax.random.split(jax.random.key(seed), 6)
    part_splits = jax.random.split(jax.random.fold_in(arg_keys[5], part), 6)
    return {
        "images": draw_images(jax.random.fold_in(jax.random.fold_in(arg_keys[5], part), 71), part),
        "mask_bits": set_ends(jax.random.randint(part_splits[1], (BANDS, PIECES, ROWS, COLS), 0, 16), jax.random.fold_in(part_splits[1], 1), 0, 15).astype(jnp.int32),
        "visit_weight": jnp.clip(jnp.exp(math.log(4.0) - 1.3862944 * jax.random.uniform(part_splits[2], (BANDS, PIECES), jnp.float32) ** block_scale(part_splits[2], (BANDS, PIECES), ((0, 2), (1, 4)), -0.2, 0.2)), 1.0, 4.0).astype(jnp.bfloat16),
        "intersection": draw_intersection(jax.random.fold_in(jax.random.fold_in(arg_keys[5], part), 71), part),
        "patch_owner": jax.random.permutation(part_splits[4], PATCHES).astype(jnp.int32),
    }


basis_rows = (0, 0, 1, 0, 2, 1)
basis_cols = (0, 1, 0, 2, 0, 1)

def kernel_taps():
    offsets = jnp.arange(2 * HALF + 1).astype(jnp.float32) - HALF
    gaussian = jnp.exp(-offsets * offsets / 18.0)
    centre = jnp.sum(offsets * offsets * gaussian * gaussian) / jnp.sum(gaussian * gaussian)
    tap_table = jnp.stack([gaussian, offsets * gaussian, (offsets * offsets - centre) * gaussian])
    tap_table = tap_table / jnp.sqrt(lax.optimization_barrier(jnp.sum(tap_table * tap_table, axis=1, keepdims=True)))
    return tap_table.astype(jnp.bfloat16)

def solve_small(matrix, right_side):
    dimension = matrix.shape[-1]
    augmented = jnp.concatenate([matrix, right_side[..., None]], axis=-1)
    for column in range(dimension):
        pivot_row = augmented[..., column, :] / augmented[..., column, column:column + 1]
        augmented = augmented - augmented[..., :, column:column + 1] * pivot_row[..., None, :]
        augmented = augmented.at[..., column, :].set(pivot_row)
    return augmented[..., :, dimension]

def reference(images, mask_bits, visit_weight, intersection, patch_owner):
    usable = (jnp.bitwise_and(mask_bits, 3) != 3).astype(jnp.bfloat16)
    weighted = visit_weight[:, :, None, None] * usable
    patch_ids = intersection[:, 0]
    band_count = images.shape[0]
    zero_planes = jnp.zeros((band_count, PATCHES, ROWS, COLS), jnp.float32)

    def accumulate(carry, piece_index):
        numerator, denominator = carry
        weight_plane = lax.dynamic_index_in_dim(weighted, piece_index, 1, keepdims=False).astype(jnp.float32)
        image_plane = lax.dynamic_index_in_dim(images, piece_index, 1, keepdims=False).astype(jnp.float32)
        target = patch_ids[piece_index]
        numerator = numerator.at[:, target].add(weight_plane * image_plane)
        denominator = denominator.at[:, target].add(weight_plane)
        return ((numerator, denominator), None)
    (numerator, denominator), _ = lax.scan(accumulate, (zero_planes, zero_planes), jnp.arange(PIECES))
    coadd_patch = (numerator / jnp.maximum(denominator, 1.0)).astype(jnp.bfloat16)
    coadd_image = jnp.zeros_like(coadd_patch).at[:, patch_owner].set(coadd_patch)
    taps_float = kernel_taps().astype(jnp.float32)

    def per_piece(piece_index):
        template = jnp.take(coadd_patch, patch_ids[piece_index], axis=1).astype(jnp.float32)
        padded = jnp.pad(template, ((0, 0), (HALF, HALF), (0, 0)))
        smooth = jnp.zeros((3, band_count, ROWS, COLS), jnp.float32)
        for offset_index in range(2 * HALF + 1):
            smooth = smooth + taps_float[:, offset_index, None, None, None] * padded[None, :, offset_index:offset_index + ROWS]
        smooth = smooth.astype(jnp.bfloat16)
        widened = jnp.pad(smooth.astype(jnp.float32), ((0, 0), (0, 0), (0, 0), (HALF, HALF)))
        planes = []
        for basis_index in range(BASES):
            total = jnp.zeros((band_count, ROWS, COLS), jnp.float32)
            for offset_index in range(2 * HALF + 1):
                total = total + taps_float[basis_cols[basis_index], offset_index] * widened[basis_rows[basis_index], :, :, offset_index:offset_index + COLS]
            planes.append(total.astype(jnp.bfloat16))
        basis = jnp.stack(planes).astype(jnp.float32)
        usable_plane = lax.dynamic_index_in_dim(usable, piece_index, 1, keepdims=False).astype(jnp.float32)
        science = lax.dynamic_index_in_dim(images, piece_index, 1, keepdims=False).astype(jnp.float32)
        masked = basis * usable_plane[None]
        normal = jnp.einsum('abyx,cbyx->bac', masked, basis, precision=lax.Precision.HIGHEST)
        right_side = jnp.einsum('abyx,byx->ba', masked, science, precision=lax.Precision.HIGHEST)
        coefficients = solve_small(normal + jnp.eye(BASES, dtype=jnp.float32), right_side)
        fitted = jnp.einsum('ba,abyx->byx', coefficients, basis, precision=lax.Precision.HIGHEST)
        return (science - fitted).astype(jnp.bfloat16)
    difference = jnp.transpose(lax.map(per_piece, jnp.arange(PIECES)), (1, 0, 2, 3))
    return (coadd_image, difference)
```

```python
import functools

import jax
import jax.numpy as jnp
import numpy as np
from jax import lax
from jax.experimental import pallas as pl
from jax.experimental.pallas import tpu as pltpu
from jax.sharding import PartitionSpec as P

BASES = 6
HALF = 9
TILE = 16

basis_rows = (0, 0, 1, 0, 2, 1)
basis_cols = (0, 1, 0, 2, 0, 1)
pairs = tuple((a, c) for a in range(BASES) for c in range(a, BASES))
MESH = pl.DeviceIdType.MESH
F32 = jnp.float32
BF16 = jnp.bfloat16


def kernel_taps():
    offsets = np.arange(2 * HALF + 1).astype(np.float32) - HALF
    gaussian = np.exp(-offsets * offsets / np.float32(18.0))
    centre = np.sum(offsets * offsets * gaussian * gaussian) / np.sum(gaussian * gaussian)
    table = np.stack([gaussian, offsets * gaussian, (offsets * offsets - centre) * gaussian])
    table = table / np.sqrt(np.sum(table * table, axis=1, keepdims=True))
    return table.astype(BF16).astype(np.float32)


def band_matrix(table, lead, trail, displace):
    index = np.arange(trail)[None, :] - np.arange(lead)[:, None] + displace
    inside = (index >= 0) & (index <= 2 * HALF)
    return np.where(inside[None], table[:, np.clip(index, 0, 2 * HALF)], 0.0)


def gather_matrix():
    result = np.zeros((BASES * 8, (len(pairs) + BASES) * TILE), np.float32)
    for n, (a, c) in enumerate(pairs):
        result[a * 8 + c, n * TILE : (n + 1) * TILE] = 1.0
        result[c * 8 + a, n * TILE : (n + 1) * TILE] = 1.0
    for a in range(BASES):
        n = len(pairs) + a
        result[a * 8 + 6, n * TILE : (n + 1) * TILE] = 1.0
    return result


def iota(shape, dim):
    return lax.broadcasted_iota(jnp.int32, shape, dim)


def nn(a, b):
    return jnp.dot(a, b, preferred_element_type=F32)


def nt(a, b, precision=None):
    return lax.dot_general(
        a, b, (((1,), (1,)), ((), ())), preferred_element_type=F32, precision=precision
    )


def kernel(
    visits, strips, distinct,
    images, masks, weight, cross, owner, cross_scalar, across_in, vertical_in, collect_in,
    coadd_out, diff_out,
    image_v, mask_v, across, vertical, collect, use, use_image, sums, send, recv, gath,
    basis, prods, small, small_in, diff_v,
    in_sem, const_sem, out_sem, rs_send, rs_recv, ag_send, ag_recv, halo_send, halo_recv,
    st_send, st_recv,
):
    pieces, rows, cols = images.shape[1:]
    blocks = rows // TILE
    span = pieces * TILE
    me = lax.axis_index("visit")
    strip = lax.axis_index("strip")

    loads = []
    for t in range(blocks):
        piece_rows = pl.ds(t * TILE, TILE)
        loads.append((
            pltpu.make_async_copy(masks.at[0, :, piece_rows, :], mask_v.at[t], in_sem.at[0, t]),
            pltpu.make_async_copy(images.at[0, :, piece_rows, :], image_v.at[t], in_sem.at[1, t]),
        ))
    constants = [
        pltpu.make_async_copy(across_in, across, const_sem.at[0]),
        pltpu.make_async_copy(vertical_in, vertical, const_sem.at[1]),
        pltpu.make_async_copy(collect_in, collect, const_sem.at[2]),
    ]
    for pair in loads:
        for copy in pair:
            copy.start()
    for copy in constants:
        copy.start()

    barrier = pltpu.get_barrier_semaphore()
    above = strip > 0
    below = strip < strips - 1

    def other_visit(k):
        return lax.rem(me + k, visits)

    for k in range(visits):
        for hop in range(strips):
            if k == 0 and hop == 0:
                continue
            target = {"visit": other_visit(k), "strip": lax.rem(strip + hop, strips)}
            pl.semaphore_signal(barrier, inc=1, device_id=target, device_id_type=MESH)

    position = jnp.zeros((pieces, 1), jnp.int32)
    for p in range(visits):
        position = position + jnp.where(cross[...] == p, owner[p], 0)
    one_hot = (position == iota((pieces, 128), 1)).astype(F32).astype(BF16)
    eq = (jnp.right_shift(iota((visits * TILE, 128), 0), 4) == iota((visits * TILE, 128), 1))
    spread = nt(eq.astype(F32).astype(BF16), one_hot)
    spread = (spread * weight[...].astype(F32)).astype(BF16)
    e2 = iota((pieces, span), 0) == jnp.right_shift(iota((pieces, span), 1), 4)
    wide = nn(spread, e2.astype(F32).astype(BF16))
    same = (iota((visits * TILE, span), 0) & (TILE - 1)) == (
        iota((visits * TILE, span), 1) & (TILE - 1)
    )
    adder = jnp.where(same, wide, 0.0).astype(BF16)
    e_rows = jnp.right_shift(iota((span, 128), 0), 4) == iota((span, 128), 1)
    e_rows = e_rows.astype(F32).astype(BF16)
    row_hot = nn(e_rows[:, :pieces], one_hot)

    seats = [owner[cross_scalar[j, 0]] for j in range(pieces)]
    slots = [jnp.int32(0)] * distinct
    rank = jnp.int32(0)
    for q in range(visits):
        present = jnp.int32(0)
        for j in range(pieces):
            present = present | jnp.where(seats[j] == q, 1, 0)
        for d in range(distinct):
            slots[d] = slots[d] + jnp.where((present == 1) & (rank == d), q, 0)
        rank = rank + present

    for t in range(blocks):
        for copy in loads[t]:
            copy.wait()
        usable = ((mask_v[t].reshape(span, cols) & 3) != 3).astype(F32).astype(BF16)
        masked = usable * image_v[t].reshape(span, cols)
        lanes = pl.ds(t * cols, cols)
        use[:, lanes] = usable
        use_image[:, lanes] = masked
        for part, value in enumerate((masked, usable)):
            total = nn(adder, value)
            for q in range(visits):
                block = total[q * TILE : (q + 1) * TILE]
                sums[q, part, pl.ds(t * TILE, TILE), :] = block
                send[q, part, pl.ds(t * TILE, TILE), :] = block.astype(BF16)

    pl.semaphore_wait(barrier, visits * strips - 1)

    copies = []
    for k in range(1, visits):
        copies.append(pltpu.make_async_remote_copy(
            src_ref=send.at[other_visit(k)], dst_ref=recv.at[k - 1],
            send_sem=rs_send.at[k - 1], recv_sem=rs_recv.at[k - 1],
            device_id={"visit": other_visit(k)}, device_id_type=MESH,
        ))
    for copy in copies:
        copy.start()

    @pl.when(jnp.logical_not(above))
    def _():
        gath[:, pl.ds(0, TILE), :] = jnp.zeros((visits, TILE, cols), BF16)

    @pl.when(jnp.logical_not(below))
    def _():
        gath[:, pl.ds(TILE + rows, TILE), :] = jnp.zeros((visits, TILE, cols), BF16)

    numerator = sums[me, 0]
    denominator = sums[me, 1]
    for k in range(1, visits):
        copies[k - 1].wait_recv()
        numerator = numerator + recv[k - 1, 0].astype(F32)
        denominator = denominator + recv[k - 1, 1].astype(F32)
    coadd = (numerator / jnp.maximum(denominator, 1.0)).astype(BF16)
    gath[me, pl.ds(TILE, rows), :] = coadd

    mains = []
    for k in range(1, visits):
        place = gath.at[me, pl.ds(TILE, rows)]
        mains.append(pltpu.make_async_remote_copy(
            src_ref=place, dst_ref=place,
            send_sem=ag_send.at[k - 1], recv_sem=ag_recv.at[k - 1],
            device_id={"visit": other_visit(k)}, device_id_type=MESH,
        ))
    downs, ups = [], []
    for k in range(visits):
        downs.append(pltpu.make_async_remote_copy(
            src_ref=gath.at[me, pl.ds(rows, TILE)], dst_ref=gath.at[me, pl.ds(0, TILE)],
            send_sem=halo_send.at[0, k], recv_sem=halo_recv.at[0, k],
            device_id={"visit": other_visit(k), "strip": lax.rem(strip + 1, strips)},
            device_id_type=MESH,
        ))
        ups.append(pltpu.make_async_remote_copy(
            src_ref=gath.at[me, pl.ds(TILE, TILE)], dst_ref=gath.at[me, pl.ds(TILE + rows, TILE)],
            send_sem=halo_send.at[1, k], recv_sem=halo_recv.at[1, k],
            device_id={"visit": other_visit(k), "strip": lax.rem(strip + strips - 1, strips)},
            device_id_type=MESH,
        ))
    for copy in mains:
        copy.start()

    @pl.when(below)
    def _():
        for copy in downs:
            copy.start()

    @pl.when(above)
    def _():
        for copy in ups:
            copy.start()

    coadd_copy = pltpu.make_async_copy(
        gath.at[me, pl.ds(TILE, rows)], coadd_out.at[0, 0], out_sem.at[0]
    )
    coadd_copy.start()
    for copy in constants:
        copy.wait()
    for copy in mains:
        copy.wait_recv()

    @pl.when(above)
    def _():
        for copy in downs:
            copy.wait_recv()

    @pl.when(below)
    def _():
        for copy in ups:
            copy.wait_recv()

    for d in range(distinct):
        template = gath[slots[d]]
        smooth = nn(vertical[...], template).astype(BF16)
        planes = [None] * BASES
        for c in range(3):
            taken = [a for a in range(BASES) if basis_cols[a] == c]
            product = nn(smooth[: len(taken) * rows], across[c]).astype(BF16)
            for a in taken:
                r = basis_rows[a]
                planes[a] = product[r * rows : (r + 1) * rows]
        for a in range(BASES):
            for t in range(blocks):
                basis[d, pl.ds(a * TILE, TILE), pl.ds(t * cols, cols)] = planes[a][
                    t * TILE : (t + 1) * TILE
                ]
        for n, (a, c) in enumerate(pairs):
            product = planes[a] * planes[c]
            for t in range(blocks):
                prods[d, pl.ds(n * TILE, TILE), pl.ds(t * cols, cols)] = product[
                    t * TILE : (t + 1) * TILE
                ]

    def member(d):
        chosen = jnp.where(iota((span, 128), 1) == slots[d], row_hot, 0.0)
        return jnp.sum(chosen, axis=1, keepdims=True)

    def summed(values):
        return jnp.sum(values.reshape(pieces, TILE, values.shape[1]), axis=1)

    def keep(width):
        return (iota((span, width), 0) & (TILE - 1)) == (iota((span, width), 1) & (TILE - 1))

    wide_n = len(pairs) * TILE
    wide_b = BASES * TILE
    normal = jnp.zeros((pieces, wide_n), F32)
    right = jnp.zeros((pieces, wide_b), F32)
    for d in range(distinct):
        mine = member(d)
        normal = normal + summed(jnp.where(keep(wide_n), nt(use[...], prods[d]), 0.0) * mine)
        right = right + summed(jnp.where(keep(wide_b), nt(use_image[...], basis[d]), 0.0) * mine)
    system = nt(collect[:, :wide_n], normal, lax.Precision.HIGHEST) + nt(
        collect[:, wide_n:], right, lax.Precision.HIGHEST
    )
    small[...] = jnp.concatenate(
        [system, jnp.zeros((BASES * 8, 128 - pieces), F32)], axis=1
    )
    exchanges = []
    for hop in range(1, strips):
        exchanges.append(pltpu.make_async_remote_copy(
            src_ref=small, dst_ref=small_in.at[hop - 1],
            send_sem=st_send.at[hop - 1], recv_sem=st_recv.at[hop - 1],
            device_id={"strip": lax.rem(strip + hop, strips)}, device_id_type=MESH,
        ))
    for copy in exchanges:
        copy.start()
    full = small[...]
    for hop in range(1, strips):
        exchanges[hop - 1].wait_recv()
        full = full + small_in[hop - 1]

    line = iota((8, 128), 0)
    table = [
        full[a * 8 : (a + 1) * 8] + jnp.where(line == a, 1.0, 0.0) for a in range(BASES)
    ]
    for column in range(BASES):
        pivot = table[column] / table[column][column : column + 1]
        for i in range(BASES):
            if i != column:
                table[i] = table[i] - table[i][column : column + 1] * pivot
        table[column] = pivot
    found = jnp.zeros((8, 128), F32)
    for a in range(BASES):
        found = found + jnp.where(line == a, table[a][BASES : BASES + 1], 0.0)
    high = found.astype(BF16).astype(F32)
    low = found - high
    both = jnp.concatenate([high, low], axis=0).astype(BF16)
    by_row = nt(e_rows, both).astype(BF16)
    wide_c = 2 * wide_b
    column = iota((16, wide_c), 1)
    source = jnp.where(
        column < wide_b, jnp.right_shift(column, 4), jnp.right_shift(column - wide_b, 4) + 8
    )
    e3 = (source == iota((16, wide_c), 0)).astype(F32).astype(BF16)
    mixer = jnp.where(keep(wide_c), nn(by_row, e3), 0.0)
    mixers = [(mixer * member(d)).astype(BF16) for d in range(distinct)]
    stores = []
    for t in range(blocks):
        lanes = pl.ds(t * cols, cols)
        fitted = jnp.zeros((span, cols), F32)
        for d in range(distinct):
            planes = basis[d, :, lanes]
            fitted = fitted + nn(mixers[d], jnp.concatenate([planes, planes], axis=0))
        result = (image_v[t].reshape(span, cols).astype(F32) - fitted).astype(BF16)
        diff_v[t] = result.reshape(pieces, TILE, cols)
        copy = pltpu.make_async_copy(
            diff_v.at[t], diff_out.at[0, :, pl.ds(t * TILE, TILE), :], out_sem.at[1 + t]
        )
        copy.start()
        stores.append(copy)

    for copy in copies + mains + exchanges:
        copy.wait_send()

    @pl.when(below)
    def _():
        for copy in downs:
            copy.wait_send()

    @pl.when(above)
    def _():
        for copy in ups:
            copy.wait_send()

    coadd_copy.wait()
    for copy in stores:
        copy.wait()


def body(visits, strips, images, mask_bits, visit_weight, intersection, patch_owner):
    _, pieces, rows, cols = images.shape
    blocks = rows // TILE
    distinct = max(1, patch_owner.shape[0] // 2)
    span = pieces * TILE
    taps = kernel_taps()
    across = jnp.asarray(np.transpose(band_matrix(taps, cols, cols, HALF), (0, 2, 1)), BF16)
    vertical = jnp.asarray(
        band_matrix(taps, rows, rows + 2 * TILE, HALF - TILE).reshape(3 * rows, rows + 2 * TILE),
        BF16,
    )
    collect = jnp.asarray(gather_matrix())
    anywhere = pl.BlockSpec(memory_space=pl.ANY)
    vmem = pl.BlockSpec(memory_space=pltpu.VMEM)
    smem = pl.BlockSpec(memory_space=pltpu.SMEM)
    dma = pltpu.SemaphoreType.DMA
    peers = max(1, visits - 1)
    return pl.pallas_call(
        functools.partial(kernel, visits, strips, distinct),
        out_shape=(
            jax.ShapeDtypeStruct((1, 1, rows, cols), BF16),
            jax.ShapeDtypeStruct(images.shape, BF16),
        ),
        in_specs=[anywhere, anywhere, vmem, vmem, smem, smem, anywhere, anywhere, anywhere],
        out_specs=(anywhere, anywhere),
        scratch_shapes=[
            pltpu.VMEM((blocks, pieces, TILE, cols), BF16),
            pltpu.VMEM((blocks, pieces, TILE, cols), jnp.int32),
            pltpu.VMEM(across.shape, BF16),
            pltpu.VMEM(vertical.shape, BF16),
            pltpu.VMEM(collect.shape, F32),
            pltpu.VMEM((span, blocks * cols), BF16),
            pltpu.VMEM((span, blocks * cols), BF16),
            pltpu.VMEM((visits, 2, rows, cols), F32),
            pltpu.VMEM((visits, 2, rows, cols), BF16),
            pltpu.VMEM((peers, 2, rows, cols), BF16),
            pltpu.VMEM((visits, rows + 2 * TILE, cols), BF16),
            pltpu.VMEM((distinct, BASES * TILE, blocks * cols), BF16),
            pltpu.VMEM((distinct, len(pairs) * TILE, blocks * cols), BF16),
            pltpu.VMEM((BASES * 8, 128), F32),
            pltpu.VMEM((max(1, strips - 1), BASES * 8, 128), F32),
            pltpu.VMEM((blocks, pieces, TILE, cols), BF16),
            dma((2, blocks)),
            dma((3,)),
            dma((1 + blocks,)),
            dma((peers,)),
            dma((peers,)),
            dma((peers,)),
            dma((peers,)),
            dma((2, visits)),
            dma((2, visits)),
            dma((max(1, strips - 1),)),
            dma((max(1, strips - 1),)),
        ],
        compiler_params=pltpu.CompilerParams(
            collective_id=0, has_side_effects=True, vmem_limit_bytes=48 * 1024 * 1024
        ),
        name="coadd_difference",
    )(
        images, mask_bits, visit_weight, intersection, patch_owner, intersection,
        across, vertical, collect,
    )


def solution(mesh):
    in_specs = (
        P("band", ("groups", "visit"), "strip", None),
        P("band", ("groups", "visit"), "strip", None),
        P("band", ("groups", "visit")),
        P(("groups", "visit"), None),
        P("groups"),
    )
    out_specs = (
        P("band", ("groups", "visit"), "strip", None),
        P("band", ("groups", "visit"), "strip", None),
    )
    step = functools.partial(body, mesh.shape["visit"], mesh.shape["strip"])
    return jax.shard_map(step, mesh=mesh, in_specs=in_specs, out_specs=out_specs, check_vma=False)
```

```python
import functools

import jax
import jax.numpy as jnp
import numpy as np
from jax import lax
from jax.experimental import pallas as pl
from jax.experimental.pallas import tpu as pltpu
from jax.sharding import PartitionSpec as P

BASES = 6
HALF = 9
TILE = 16

basis_rows = (0, 0, 1, 0, 2, 1)
basis_cols = (0, 1, 0, 2, 0, 1)
pairs = tuple((a, c) for a in range(BASES) for c in range(a, BASES))
MESH = pl.DeviceIdType.MESH
F32 = jnp.float32
BF16 = jnp.bfloat16


def kernel_taps():
    offsets = np.arange(2 * HALF + 1).astype(np.float32) - HALF
    gaussian = np.exp(-offsets * offsets / np.float32(18.0))
    centre = np.sum(offsets * offsets * gaussian * gaussian) / np.sum(gaussian * gaussian)
    table = np.stack([gaussian, offsets * gaussian, (offsets * offsets - centre) * gaussian])
    table = table / np.sqrt(np.sum(table * table, axis=1, keepdims=True))
    return table.astype(BF16).astype(np.float32)


def band_matrix(table, lead, trail, displace):
    index = np.arange(trail)[None, :] - np.arange(lead)[:, None] + displace
    inside = (index >= 0) & (index <= 2 * HALF)
    return np.where(inside[None], table[:, np.clip(index, 0, 2 * HALF)], 0.0)


def gather_matrix():
    result = np.zeros((BASES * 8, (len(pairs) + BASES) * TILE), np.float32)
    for n, (a, c) in enumerate(pairs):
        result[a * 8 + c, n * TILE : (n + 1) * TILE] = 1.0
        result[c * 8 + a, n * TILE : (n + 1) * TILE] = 1.0
    for a in range(BASES):
        n = len(pairs) + a
        result[a * 8 + 6, n * TILE : (n + 1) * TILE] = 1.0
    return result


def iota(shape, dim):
    return lax.broadcasted_iota(jnp.int32, shape, dim)


def nn(a, b):
    return jnp.dot(a, b, preferred_element_type=F32)


def nt(a, b, precision=None):
    return lax.dot_general(
        a, b, (((1,), (1,)), ((), ())), preferred_element_type=F32, precision=precision
    )


def kernel(
    visits, strips, distinct,
    images, masks, weight, cross, owner, cross_scalar, across_in, vertical_in, collect_in,
    coadd_out, image_v, basis, mixers,
    mask_v, across, vertical, collect, use, use_image, sums, send, recv, gath,
    prods, small, small_in,
    in_sem, const_sem, rs_send, rs_recv, ag_send, ag_recv, halo_send, halo_recv,
    st_send, st_recv,
):
    pieces, rows, cols = images.shape[1:]
    blocks = rows // TILE
    span = pieces * TILE
    order = [0] + ([blocks - 1] if blocks > 1 else []) + list(range(1, blocks - 1))
    me = lax.axis_index("visit")
    strip = lax.axis_index("strip")

    loads = {}
    for t in order:
        piece_rows = pl.ds(t * TILE, TILE)
        loads[t] = ((
            pltpu.make_async_copy(masks.at[0, :, piece_rows, :], mask_v.at[t], in_sem.at[0, t]),
            pltpu.make_async_copy(images.at[0, :, piece_rows, :], image_v.at[t], in_sem.at[1, t]),
        ))
    constants = [
        pltpu.make_async_copy(across_in, across, const_sem.at[0]),
        pltpu.make_async_copy(vertical_in, vertical, const_sem.at[1]),
        pltpu.make_async_copy(collect_in, collect, const_sem.at[2]),
    ]
    for t in order:
        for copy in loads[t]:
            copy.start()
    for copy in constants:
        copy.start()

    barrier = pltpu.get_barrier_semaphore()
    above = strip > 0
    below = strip < strips - 1

    def other_visit(k):
        return lax.rem(me + k, visits)

    for k in range(visits):
        for hop in range(strips):
            if k == 0 and hop == 0:
                continue
            target = {"visit": other_visit(k), "strip": lax.rem(strip + hop, strips)}
            pl.semaphore_signal(barrier, inc=1, device_id=target, device_id_type=MESH)

    position = jnp.zeros((1, pieces), jnp.int32)
    for p in range(visits):
        position = position + jnp.where(cross[...] == p, owner[p], 0)
    one_hot = (position == iota((128, pieces), 0)).astype(F32).astype(BF16)
    eq = (jnp.right_shift(iota((visits * TILE, 128), 0), 4) == iota((visits * TILE, 128), 1))
    spread = nn(eq.astype(F32).astype(BF16), one_hot)
    spread = (spread * weight[...].astype(F32)).astype(BF16)
    e2 = iota((pieces, span), 0) == jnp.right_shift(iota((pieces, span), 1), 4)
    wide = nn(spread, e2.astype(F32).astype(BF16))
    same = (iota((visits * TILE, span), 0) & (TILE - 1)) == (
        iota((visits * TILE, span), 1) & (TILE - 1)
    )
    adder = jnp.where(same, wide, 0.0).astype(BF16)
    e_rows = jnp.right_shift(iota((span, 128), 0), 4) == iota((span, 128), 1)
    e_rows = e_rows.astype(F32).astype(BF16)
    row_hot = nt(e_rows[:, :pieces], one_hot)

    seats = [owner[cross_scalar[0, j]] for j in range(pieces)]
    slots = [jnp.int32(0)] * distinct
    rank = jnp.int32(0)
    for q in range(visits):
        present = jnp.int32(0)
        for j in range(pieces):
            present = present | jnp.where(seats[j] == q, 1, 0)
        for d in range(distinct):
            slots[d] = slots[d] + jnp.where((present == 1) & (rank == d), q, 0)
        rank = rank + present

    for t in order:
        for copy in loads[t]:
            copy.wait()
        usable = ((mask_v[t].reshape(span, cols) & 3) != 3).astype(F32).astype(BF16)
        masked = usable * image_v[t].reshape(span, cols)
        lanes = pl.ds(t * cols, cols)
        use[:, lanes] = usable
        use_image[:, lanes] = masked
        for part, value in enumerate((masked, usable)):
            total = nn(adder, value)
            for q in range(visits):
                block = total[q * TILE : (q + 1) * TILE]
                sums[t, q, part] = block
                send[t, q, part] = block.astype(BF16)

    pl.semaphore_wait(barrier, visits * strips - 1)

    reduces = {}
    for t in order:
        for k in range(visits - 1, 0, -1):
            reduces[t, k] = pltpu.make_async_remote_copy(
                src_ref=send.at[t, other_visit(k)], dst_ref=recv.at[t, k - 1],
                send_sem=rs_send.at[t, k - 1], recv_sem=rs_recv.at[t, k - 1],
                device_id={"visit": other_visit(k)}, device_id_type=MESH,
            )
            reduces[t, k].start()

    @pl.when(jnp.logical_not(above))
    def _():
        gath[:, pl.ds(0, TILE), :] = jnp.zeros((visits, TILE, cols), BF16)

    @pl.when(jnp.logical_not(below))
    def _():
        gath[:, pl.ds(TILE + rows, TILE), :] = jnp.zeros((visits, TILE, cols), BF16)

    downs, ups = [], []
    for k in range(visits):
        downs.append(pltpu.make_async_remote_copy(
            src_ref=gath.at[me, pl.ds(rows, TILE)], dst_ref=gath.at[me, pl.ds(0, TILE)],
            send_sem=halo_send.at[0, k], recv_sem=halo_recv.at[0, k],
            device_id={"visit": other_visit(k), "strip": lax.rem(strip + 1, strips)},
            device_id_type=MESH,
        ))
        ups.append(pltpu.make_async_remote_copy(
            src_ref=gath.at[me, pl.ds(TILE, TILE)], dst_ref=gath.at[me, pl.ds(TILE + rows, TILE)],
            send_sem=halo_send.at[1, k], recv_sem=halo_recv.at[1, k],
            device_id={"visit": other_visit(k), "strip": lax.rem(strip + strips - 1, strips)},
            device_id_type=MESH,
        ))
    gathers = {}
    for t in order:
        numerator = sums[t, me, 0]
        denominator = sums[t, me, 1]
        for k in range(1, visits):
            reduces[t, k].wait_recv()
            numerator = numerator + recv[t, k - 1, 0].astype(F32)
            denominator = denominator + recv[t, k - 1, 1].astype(F32)
        coadd = (numerator / jnp.maximum(denominator, 1.0)).astype(BF16)
        gath[me, pl.ds(TILE + t * TILE, TILE), :] = coadd
        coadd_out[pl.ds(t * TILE, TILE), :] = coadd
        for k in range(1, visits):
            place = gath.at[me, pl.ds(TILE + t * TILE, TILE)]
            gathers[t, k] = pltpu.make_async_remote_copy(
                src_ref=place, dst_ref=place,
                send_sem=ag_send.at[t, k - 1], recv_sem=ag_recv.at[t, k - 1],
                device_id={"visit": other_visit(k)}, device_id_type=MESH,
            )
            gathers[t, k].start()

        if t == blocks - 1:
            @pl.when(below)
            def _():
                for copy in downs:
                    copy.start()

        if t == 0:
            @pl.when(above)
            def _():
                for copy in ups:
                    copy.start()

    for copy in constants:
        copy.wait()

    @pl.when(above)
    def _():
        for copy in downs:
            copy.wait_recv()

    @pl.when(below)
    def _():
        for copy in ups:
            copy.wait_recv()

    for t in order:
        for k in range(1, visits):
            gathers[t, k].wait_recv()

    for d in range(distinct):
        template = gath[slots[d]]
        smooth = nn(vertical[...], template).astype(BF16)
        planes = [None] * BASES
        for c in range(3):
            taken = [a for a in range(BASES) if basis_cols[a] == c]
            product = nn(smooth[: len(taken) * rows], across[c]).astype(BF16)
            for a in taken:
                r = basis_rows[a]
                planes[a] = product[r * rows : (r + 1) * rows]
        for a in range(BASES):
            for t in range(blocks):
                basis[d, pl.ds(a * TILE, TILE), pl.ds(t * cols, cols)] = planes[a][
                    t * TILE : (t + 1) * TILE
                ]
        for n, (a, c) in enumerate(pairs):
            product = planes[a] * planes[c]
            for t in range(blocks):
                prods[d, pl.ds(n * TILE, TILE), pl.ds(t * cols, cols)] = product[
                    t * TILE : (t + 1) * TILE
                ]

    def member(d):
        chosen = jnp.where(iota((span, 128), 1) == slots[d], row_hot, 0.0)
        return jnp.sum(chosen, axis=1, keepdims=True)

    def summed(values):
        return jnp.sum(values.reshape(pieces, TILE, values.shape[1]), axis=1)

    def keep(width):
        return (iota((span, width), 0) & (TILE - 1)) == (iota((span, width), 1) & (TILE - 1))

    wide_n = len(pairs) * TILE
    wide_b = BASES * TILE
    normal = jnp.zeros((pieces, wide_n), F32)
    right = jnp.zeros((pieces, wide_b), F32)
    for d in range(distinct):
        mine = member(d)
        normal = normal + summed(jnp.where(keep(wide_n), nt(use[...], prods[d]), 0.0) * mine)
        right = right + summed(jnp.where(keep(wide_b), nt(use_image[...], basis[d]), 0.0) * mine)
    system = nt(collect[:, :wide_n], normal, lax.Precision.HIGHEST) + nt(
        collect[:, wide_n:], right, lax.Precision.HIGHEST
    )
    small[...] = jnp.concatenate(
        [system, jnp.zeros((BASES * 8, 128 - pieces), F32)], axis=1
    )
    exchanges = []
    for hop in range(1, strips):
        exchanges.append(pltpu.make_async_remote_copy(
            src_ref=small, dst_ref=small_in.at[hop - 1],
            send_sem=st_send.at[hop - 1], recv_sem=st_recv.at[hop - 1],
            device_id={"strip": lax.rem(strip + hop, strips)}, device_id_type=MESH,
        ))
    for copy in exchanges:
        copy.start()
    full = small[...]
    for hop in range(1, strips):
        exchanges[hop - 1].wait_recv()
        full = full + small_in[hop - 1]

    line = iota((8, 128), 0)
    table = [
        full[a * 8 : (a + 1) * 8] + jnp.where(line == a, 1.0, 0.0) for a in range(BASES)
    ]
    for column in range(BASES):
        pivot = table[column] / table[column][column : column + 1]
        for i in range(BASES):
            if i != column:
                table[i] = table[i] - table[i][column : column + 1] * pivot
        table[column] = pivot
    found = jnp.zeros((8, 128), F32)
    for a in range(BASES):
        found = found + jnp.where(line == a, table[a][BASES : BASES + 1], 0.0)
    high = found.astype(BF16).astype(F32)
    low = found - high
    both = jnp.concatenate([high, low], axis=0).astype(BF16)
    by_row = nt(e_rows, both).astype(BF16)
    wide_c = 2 * wide_b
    column = iota((16, wide_c), 1)
    source = jnp.where(
        column < wide_b, jnp.right_shift(column, 4), jnp.right_shift(column - wide_b, 4) + 8
    )
    e3 = (source == iota((16, wide_c), 0)).astype(F32).astype(BF16)
    mixer = jnp.where(keep(wide_c), nn(by_row, e3), 0.0)
    for d in range(distinct):
        mixers[d] = (mixer * member(d)).astype(BF16)

    for copy in list(reduces.values()) + list(gathers.values()) + exchanges:
        copy.wait_send()

    @pl.when(below)
    def _():
        for copy in downs:
            copy.wait_send()

    @pl.when(above)
    def _():
        for copy in ups:
            copy.wait_send()


def finish(coadd_in, image_v, basis, mixers, coadd_out, diff_out, diff_v, out_sem):
    distinct = basis.shape[0]
    blocks, pieces, _, cols = image_v.shape
    span = pieces * TILE
    stores = [pltpu.make_async_copy(coadd_in, coadd_out.at[0, 0], out_sem.at[0])]
    stores[0].start()
    for t in range(blocks):
        lanes = pl.ds(t * cols, cols)
        fitted = jnp.zeros((span, cols), F32)
        for d in range(distinct):
            planes = basis[d, :, lanes]
            fitted = fitted + nn(mixers[d], jnp.concatenate([planes, planes], axis=0))
        result = (image_v[t].reshape(span, cols).astype(F32) - fitted).astype(BF16)
        diff_v[t] = result.reshape(pieces, TILE, cols)
        copy = pltpu.make_async_copy(
            diff_v.at[t], diff_out.at[0, :, pl.ds(t * TILE, TILE), :], out_sem.at[1 + t]
        )
        copy.start()
        stores.append(copy)
    for copy in stores:
        copy.wait()


def body(visits, strips, images, mask_bits, visit_weight, intersection, patch_owner):
    _, pieces, rows, cols = images.shape
    blocks = rows // TILE
    distinct = max(1, patch_owner.shape[0] // 2)
    span = pieces * TILE
    taps = kernel_taps()
    across = jnp.asarray(np.transpose(band_matrix(taps, cols, cols, HALF), (0, 2, 1)), BF16)
    vertical = jnp.asarray(
        band_matrix(taps, rows, rows + 2 * TILE, HALF - TILE).reshape(3 * rows, rows + 2 * TILE),
        BF16,
    )
    collect = jnp.asarray(gather_matrix())
    hbm = pl.BlockSpec(memory_space=pltpu.HBM)
    vmem = pl.BlockSpec(memory_space=pltpu.VMEM)
    smem = pl.BlockSpec(memory_space=pltpu.SMEM)
    dma = pltpu.SemaphoreType.DMA
    peers = max(1, visits - 1)
    cross = intersection.reshape(1, pieces)
    middle = pl.pallas_call(
        functools.partial(kernel, visits, strips, distinct),
        out_shape=(
            jax.ShapeDtypeStruct((rows, cols), BF16),
            jax.ShapeDtypeStruct((blocks, pieces, TILE, cols), BF16),
            jax.ShapeDtypeStruct((distinct, BASES * TILE, blocks * cols), BF16),
            jax.ShapeDtypeStruct((distinct, span, 2 * BASES * TILE), BF16),
        ),
        in_specs=[hbm, hbm, vmem, vmem, smem, smem, hbm, hbm, hbm],
        out_specs=(vmem, vmem, vmem, vmem),
        scratch_shapes=[
            pltpu.VMEM((blocks, pieces, TILE, cols), jnp.int32),
            pltpu.VMEM(across.shape, BF16),
            pltpu.VMEM(vertical.shape, BF16),
            pltpu.VMEM(collect.shape, F32),
            pltpu.VMEM((span, blocks * cols), BF16),
            pltpu.VMEM((span, blocks * cols), BF16),
            pltpu.VMEM((blocks, visits, 2, TILE, cols), F32),
            pltpu.VMEM((blocks, visits, 2, TILE, cols), BF16),
            pltpu.VMEM((blocks, peers, 2, TILE, cols), BF16),
            pltpu.VMEM((visits, rows + 2 * TILE, cols), BF16),
            pltpu.VMEM((distinct, len(pairs) * TILE, blocks * cols), BF16),
            pltpu.VMEM((BASES * 8, 128), F32),
            pltpu.VMEM((max(1, strips - 1), BASES * 8, 128), F32),
            dma((2, blocks)),
            dma((3,)),
            dma((blocks, peers)),
            dma((blocks, peers)),
            dma((blocks, peers)),
            dma((blocks, peers)),
            dma((2, visits)),
            dma((2, visits)),
            dma((max(1, strips - 1),)),
            dma((max(1, strips - 1),)),
        ],
        compiler_params=pltpu.CompilerParams(
            collective_id=0, has_side_effects=True, vmem_limit_bytes=40 * 1024 * 1024
        ),
        name="coadd_solve",
    )(
        images, mask_bits, visit_weight, cross, patch_owner, cross,
        across, vertical, collect,
    )
    return pl.pallas_call(
        finish,
        out_shape=(
            jax.ShapeDtypeStruct((1, 1, rows, cols), BF16),
            jax.ShapeDtypeStruct(images.shape, BF16),
        ),
        in_specs=[vmem, vmem, vmem, vmem],
        out_specs=(hbm, hbm),
        scratch_shapes=[pltpu.VMEM((blocks, pieces, TILE, cols), BF16), dma((1 + blocks,))],
        compiler_params=pltpu.CompilerParams(vmem_limit_bytes=32 * 1024 * 1024),
        name="difference",
    )(*middle)


def solution(mesh):
    in_specs = (
        P("band", ("groups", "visit"), "strip", None),
        P("band", ("groups", "visit"), "strip", None),
        P("band", ("groups", "visit")),
        P(("groups", "visit"), None),
        P("groups"),
    )
    out_specs = (
        P("band", ("groups", "visit"), "strip", None),
        P("band", ("groups", "visit"), "strip", None),
    )
    step = functools.partial(body, mesh.shape["visit"], mesh.shape["strip"])
    return jax.shard_map(step, mesh=mesh, in_specs=in_specs, out_specs=out_specs, check_vma=False)
```

```python
import functools

import jax
import jax.numpy as jnp
import numpy as np
from jax import lax
from jax.experimental import pallas as pl
from jax.experimental.pallas import tpu as pltpu
from jax.sharding import PartitionSpec as P

BASES = 6
HALF = 9
TILE = 16

basis_rows = (0, 0, 1, 0, 2, 1)
basis_cols = (0, 1, 0, 2, 0, 1)
pairs = tuple((a, c) for a in range(BASES) for c in range(a, BASES))
MESH = pl.DeviceIdType.MESH
F32 = jnp.float32
BF16 = jnp.bfloat16


def kernel_taps():
    offsets = np.arange(2 * HALF + 1).astype(np.float32) - HALF
    gaussian = np.exp(-offsets * offsets / np.float32(18.0))
    centre = np.sum(offsets * offsets * gaussian * gaussian) / np.sum(gaussian * gaussian)
    table = np.stack([gaussian, offsets * gaussian, (offsets * offsets - centre) * gaussian])
    table = table / np.sqrt(np.sum(table * table, axis=1, keepdims=True))
    return table.astype(BF16).astype(np.float32)


def band_matrix(table, lead, trail, displace):
    index = np.arange(trail)[None, :] - np.arange(lead)[:, None] + displace
    inside = (index >= 0) & (index <= 2 * HALF)
    return np.where(inside[None], table[:, np.clip(index, 0, 2 * HALF)], 0.0)


def gather_matrix():
    result = np.zeros((BASES * 8, (len(pairs) + BASES) * TILE), np.float32)
    for n, (a, c) in enumerate(pairs):
        result[a * 8 + c, n * TILE : (n + 1) * TILE] = 1.0
        result[c * 8 + a, n * TILE : (n + 1) * TILE] = 1.0
    for a in range(BASES):
        n = len(pairs) + a
        result[a * 8 + 6, n * TILE : (n + 1) * TILE] = 1.0
    return result


def iota(shape, dim):
    return lax.broadcasted_iota(jnp.int32, shape, dim)


def nn(a, b):
    return jnp.dot(a, b, preferred_element_type=F32)


def nt(a, b, precision=None):
    return lax.dot_general(
        a, b, (((1,), (1,)), ((), ())), preferred_element_type=F32, precision=precision
    )


def kernel(
    visits, strips, distinct,
    images, masks, weight, cross, owner, cross_scalar, table_in,
    coadd_out, image_v, basis, mixers,
    mask_v, tables, use, use_image, sums, send, recv, gath,
    prods, small, small_in,
    in_sem, const_sem, rs_send, rs_recv, ag_send, ag_recv, halo_send, halo_recv,
    st_send, st_recv,
):
    pieces, rows, cols = images.shape[1:]
    blocks = rows // TILE
    span = pieces * TILE
    order = [0] + ([blocks - 1] if blocks > 1 else []) + list(range(1, blocks - 1))
    me = lax.axis_index("visit")
    strip = lax.axis_index("strip")

    loads = {}
    for t in order:
        piece_rows = pl.ds(t * TILE, TILE)
        loads[t] = ((
            pltpu.make_async_copy(masks.at[0, :, piece_rows, :], mask_v.at[t], in_sem.at[0, t]),
            pltpu.make_async_copy(images.at[0, :, piece_rows, :], image_v.at[t], in_sem.at[1, t]),
        ))
    constants = [pltpu.make_async_copy(table_in, tables, const_sem)]
    for t in order:
        for copy in loads[t]:
            copy.start()
    for copy in constants:
        copy.start()

    barrier = pltpu.get_barrier_semaphore()
    above = strip > 0
    below = strip < strips - 1

    def other_visit(k):
        return lax.rem(me + k, visits)

    for k in range(visits):
        for hop in range(strips):
            if k == 0 and hop == 0:
                continue
            target = {"visit": other_visit(k), "strip": lax.rem(strip + hop, strips)}
            pl.semaphore_signal(barrier, inc=1, device_id=target, device_id_type=MESH)

    position = jnp.zeros((1, pieces), jnp.int32)
    for p in range(visits):
        position = position + jnp.where(cross[...] == p, owner[p], 0)
    one_hot = (position == iota((128, pieces), 0)).astype(F32).astype(BF16)
    eq = (jnp.right_shift(iota((visits * TILE, 128), 0), 4) == iota((visits * TILE, 128), 1))
    spread = nn(eq.astype(F32).astype(BF16), one_hot)
    spread = (spread * weight[...].astype(F32)).astype(BF16)
    e2 = iota((pieces, span), 0) == jnp.right_shift(iota((pieces, span), 1), 4)
    wide = nn(spread, e2.astype(F32).astype(BF16))
    same = (iota((visits * TILE, span), 0) & (TILE - 1)) == (
        iota((visits * TILE, span), 1) & (TILE - 1)
    )
    adder = jnp.where(same, wide, 0.0).astype(BF16)
    e_rows = jnp.right_shift(iota((span, 128), 0), 4) == iota((span, 128), 1)
    e_rows = e_rows.astype(F32).astype(BF16)
    row_hot = nt(e_rows[:, :pieces], one_hot)

    seats = [owner[cross_scalar[0, j]] for j in range(pieces)]
    slots = [jnp.int32(0)] * distinct
    rank = jnp.int32(0)
    for q in range(visits):
        present = jnp.int32(0)
        for j in range(pieces):
            present = present | jnp.where(seats[j] == q, 1, 0)
        for d in range(distinct):
            slots[d] = slots[d] + jnp.where((present == 1) & (rank == d), q, 0)
        rank = rank + present

    for t in order:
        for copy in loads[t]:
            copy.wait()
        usable = ((mask_v[t].reshape(span, cols) & 3) != 3).astype(F32).astype(BF16)
        masked = usable * image_v[t].reshape(span, cols)
        lanes = pl.ds(t * cols, cols)
        use[:, lanes] = usable
        use_image[:, lanes] = masked
        for part, value in enumerate((masked, usable)):
            total = nn(adder, value)
            for q in range(visits):
                block = total[q * TILE : (q + 1) * TILE]
                sums[t, q, part] = block
                send[t, q, part] = block.astype(BF16)

    pl.semaphore_wait(barrier, visits * strips - 1)

    reduces = {}
    for t in order:
        for k in range(visits - 1, 0, -1):
            reduces[t, k] = pltpu.make_async_remote_copy(
                src_ref=send.at[t, other_visit(k)], dst_ref=recv.at[t, k - 1],
                send_sem=rs_send.at[t, k - 1], recv_sem=rs_recv.at[t, k - 1],
                device_id={"visit": other_visit(k)}, device_id_type=MESH,
            )
            reduces[t, k].start()

    @pl.when(jnp.logical_not(above))
    def _():
        gath[:, pl.ds(0, TILE), :] = jnp.zeros((visits, TILE, cols), BF16)

    @pl.when(jnp.logical_not(below))
    def _():
        gath[:, pl.ds(TILE + rows, TILE), :] = jnp.zeros((visits, TILE, cols), BF16)

    downs, ups = [], []
    for k in range(visits):
        downs.append(pltpu.make_async_remote_copy(
            src_ref=gath.at[me, pl.ds(rows, TILE)], dst_ref=gath.at[me, pl.ds(0, TILE)],
            send_sem=halo_send.at[0, k], recv_sem=halo_recv.at[0, k],
            device_id={"visit": other_visit(k), "strip": lax.rem(strip + 1, strips)},
            device_id_type=MESH,
        ))
        ups.append(pltpu.make_async_remote_copy(
            src_ref=gath.at[me, pl.ds(TILE, TILE)], dst_ref=gath.at[me, pl.ds(TILE + rows, TILE)],
            send_sem=halo_send.at[1, k], recv_sem=halo_recv.at[1, k],
            device_id={"visit": other_visit(k), "strip": lax.rem(strip + strips - 1, strips)},
            device_id_type=MESH,
        ))
    gathers = {}
    for t in order:
        numerator = sums[t, me, 0]
        denominator = sums[t, me, 1]
        for k in range(1, visits):
            reduces[t, k].wait_recv()
            numerator = numerator + recv[t, k - 1, 0].astype(F32)
            denominator = denominator + recv[t, k - 1, 1].astype(F32)
        coadd = (numerator / jnp.maximum(denominator, 1.0)).astype(BF16)
        gath[me, pl.ds(TILE + t * TILE, TILE), :] = coadd
        coadd_out[pl.ds(t * TILE, TILE), :] = coadd
        for k in range(1, visits):
            place = gath.at[me, pl.ds(TILE + t * TILE, TILE)]
            gathers[t, k] = pltpu.make_async_remote_copy(
                src_ref=place, dst_ref=place,
                send_sem=ag_send.at[t, k - 1], recv_sem=ag_recv.at[t, k - 1],
                device_id={"visit": other_visit(k)}, device_id_type=MESH,
            )
            gathers[t, k].start()

        if t == blocks - 1:
            @pl.when(below)
            def _():
                for copy in downs:
                    copy.start()

        if t == 0:
            @pl.when(above)
            def _():
                for copy in ups:
                    copy.start()

    for copy in constants:
        copy.wait()

    @pl.when(above)
    def _():
        for copy in downs:
            copy.wait_recv()

    @pl.when(below)
    def _():
        for copy in ups:
            copy.wait_recv()

    for t in order:
        for k in range(1, visits):
            gathers[t, k].wait_recv()

    top = BASES // 2 * cols
    vertical = tables[pl.ds(top, 3 * rows), pl.ds(0, rows + 2 * TILE)]
    top = top + 3 * rows

    def across(c):
        return tables[pl.ds(c * cols, cols), pl.ds(0, cols)]

    for d in range(distinct):
        template = gath[slots[d]]
        smooth = nn(vertical, template).astype(BF16)
        planes = [None] * BASES
        for c in range(3):
            taken = [a for a in range(BASES) if basis_cols[a] == c]
            product = nn(smooth[: len(taken) * rows], across(c)).astype(BF16)
            for a in taken:
                r = basis_rows[a]
                planes[a] = product[r * rows : (r + 1) * rows]
        for a in range(BASES):
            for t in range(blocks):
                basis[d, pl.ds(a * TILE, TILE), pl.ds(t * cols, cols)] = planes[a][
                    t * TILE : (t + 1) * TILE
                ]
        for n, (a, c) in enumerate(pairs):
            product = planes[a] * planes[c]
            for t in range(blocks):
                prods[d, pl.ds(n * TILE, TILE), pl.ds(t * cols, cols)] = product[
                    t * TILE : (t + 1) * TILE
                ]

    def member(d):
        chosen = jnp.where(iota((span, 128), 1) == slots[d], row_hot, 0.0)
        return jnp.sum(chosen, axis=1, keepdims=True)

    def summed(values):
        return jnp.sum(values.reshape(pieces, TILE, values.shape[1]), axis=1)

    def keep(width):
        return (iota((span, width), 0) & (TILE - 1)) == (iota((span, width), 1) & (TILE - 1))

    wide_n = len(pairs) * TILE
    wide_b = BASES * TILE
    normal = jnp.zeros((pieces, wide_n), F32)
    right = jnp.zeros((pieces, wide_b), F32)
    for d in range(distinct):
        mine = member(d)
        normal = normal + summed(jnp.where(keep(wide_n), nt(use[...], prods[d]), 0.0) * mine)
        right = right + summed(jnp.where(keep(wide_b), nt(use_image[...], basis[d]), 0.0) * mine)
    normal_rows = tables[pl.ds(top, BASES * 8), pl.ds(0, wide_n)].astype(F32)
    right_rows = tables[pl.ds(top, BASES * 8), pl.ds(wide_n, wide_b)].astype(F32)
    system = nt(normal_rows, normal, lax.Precision.HIGHEST) + nt(
        right_rows, right, lax.Precision.HIGHEST
    )
    small[...] = jnp.concatenate(
        [system, jnp.zeros((BASES * 8, 128 - pieces), F32)], axis=1
    )
    exchanges = []
    for hop in range(1, strips):
        exchanges.append(pltpu.make_async_remote_copy(
            src_ref=small, dst_ref=small_in.at[hop - 1],
            send_sem=st_send.at[hop - 1], recv_sem=st_recv.at[hop - 1],
            device_id={"strip": lax.rem(strip + hop, strips)}, device_id_type=MESH,
        ))
    for copy in exchanges:
        copy.start()
    full = small[...]
    for hop in range(1, strips):
        exchanges[hop - 1].wait_recv()
        full = full + small_in[hop - 1]

    line = iota((8, 128), 0)
    table = [
        full[a * 8 : (a + 1) * 8] + jnp.where(line == a, 1.0, 0.0) for a in range(BASES)
    ]
    for column in range(BASES):
        pivot = table[column] / table[column][column : column + 1]
        for i in range(BASES):
            if i != column:
                table[i] = table[i] - table[i][column : column + 1] * pivot
        table[column] = pivot
    found = jnp.zeros((8, 128), F32)
    for a in range(BASES):
        found = found + jnp.where(line == a, table[a][BASES : BASES + 1], 0.0)
    high = found.astype(BF16).astype(F32)
    low = found - high
    both = jnp.concatenate([high, low], axis=0).astype(BF16)
    by_row = nt(e_rows, both).astype(BF16)
    wide_c = 2 * wide_b
    column = iota((16, wide_c), 1)
    source = jnp.where(
        column < wide_b, jnp.right_shift(column, 4), jnp.right_shift(column - wide_b, 4) + 8
    )
    e3 = (source == iota((16, wide_c), 0)).astype(F32).astype(BF16)
    mixer = jnp.where(keep(wide_c), nn(by_row, e3), 0.0)
    for d in range(distinct):
        mixers[d] = (mixer * member(d)).astype(BF16)

    for copy in list(reduces.values()) + list(gathers.values()) + exchanges:
        copy.wait_send()

    @pl.when(below)
    def _():
        for copy in downs:
            copy.wait_send()

    @pl.when(above)
    def _():
        for copy in ups:
            copy.wait_send()


def finish(coadd_in, image_v, basis, mixers, coadd_out, diff_out, diff_v, out_sem):
    distinct = basis.shape[0]
    blocks, pieces, _, cols = image_v.shape
    span = pieces * TILE
    stores = [pltpu.make_async_copy(coadd_in, coadd_out.at[0, 0], out_sem.at[0])]
    stores[0].start()
    for t in range(blocks):
        lanes = pl.ds(t * cols, cols)
        fitted = jnp.zeros((span, cols), F32)
        for d in range(distinct):
            planes = basis[d, :, lanes]
            fitted = fitted + nn(mixers[d], jnp.concatenate([planes, planes], axis=0))
        result = (image_v[t].reshape(span, cols).astype(F32) - fitted).astype(BF16)
        diff_v[t] = result.reshape(pieces, TILE, cols)
        copy = pltpu.make_async_copy(
            diff_v.at[t], diff_out.at[0, :, pl.ds(t * TILE, TILE), :], out_sem.at[1 + t]
        )
        copy.start()
        stores.append(copy)
    for copy in stores:
        copy.wait()


def body(visits, strips, images, mask_bits, visit_weight, intersection, patch_owner):
    _, pieces, rows, cols = images.shape
    blocks = rows // TILE
    distinct = max(1, patch_owner.shape[0] // 2)
    span = pieces * TILE
    taps = kernel_taps()
    collect = gather_matrix()
    width = max(collect.shape[1], cols, rows + 2 * TILE)
    width = -(-width // 128) * 128
    tables = jnp.asarray(np.concatenate([
        np.pad(part, ((0, 0), (0, width - part.shape[1])))
        for part in (
            np.transpose(band_matrix(taps, cols, cols, HALF), (0, 2, 1)).reshape(3 * cols, cols),
            band_matrix(taps, rows, rows + 2 * TILE, HALF - TILE).reshape(3 * rows, -1),
            collect,
        )
    ]), BF16)
    hbm = pl.BlockSpec(memory_space=pltpu.HBM)
    vmem = pl.BlockSpec(memory_space=pltpu.VMEM)
    smem = pl.BlockSpec(memory_space=pltpu.SMEM)
    dma = pltpu.SemaphoreType.DMA
    peers = max(1, visits - 1)
    cross = intersection.reshape(1, pieces)
    middle = pl.pallas_call(
        functools.partial(kernel, visits, strips, distinct),
        out_shape=(
            jax.ShapeDtypeStruct((rows, cols), BF16),
            jax.ShapeDtypeStruct((blocks, pieces, TILE, cols), BF16),
            jax.ShapeDtypeStruct((distinct, BASES * TILE, blocks * cols), BF16),
            jax.ShapeDtypeStruct((distinct, span, 2 * BASES * TILE), BF16),
        ),
        in_specs=[hbm, hbm, vmem, vmem, smem, smem, hbm],
        out_specs=(vmem, vmem, vmem, vmem),
        scratch_shapes=[
            pltpu.VMEM((blocks, pieces, TILE, cols), jnp.int32),
            pltpu.VMEM(tables.shape, BF16),
            pltpu.VMEM((span, blocks * cols), BF16),
            pltpu.VMEM((span, blocks * cols), BF16),
            pltpu.VMEM((blocks, visits, 2, TILE, cols), F32),
            pltpu.VMEM((blocks, visits, 2, TILE, cols), BF16),
            pltpu.VMEM((blocks, peers, 2, TILE, cols), BF16),
            pltpu.VMEM((visits, rows + 2 * TILE, cols), BF16),
            pltpu.VMEM((distinct, len(pairs) * TILE, blocks * cols), BF16),
            pltpu.VMEM((BASES * 8, 128), F32),
            pltpu.VMEM((max(1, strips - 1), BASES * 8, 128), F32),
            dma((2, blocks)),
            dma,
            dma((blocks, peers)),
            dma((blocks, peers)),
            dma((blocks, peers)),
            dma((blocks, peers)),
            dma((2, visits)),
            dma((2, visits)),
            dma((max(1, strips - 1),)),
            dma((max(1, strips - 1),)),
        ],
        compiler_params=pltpu.CompilerParams(
            collective_id=0, has_side_effects=True, vmem_limit_bytes=55_100_000
        ),
        name="coadd_solve",
    )(
        images, mask_bits, visit_weight, cross, patch_owner, cross,
        tables,
    )
    return pl.pallas_call(
        finish,
        out_shape=(
            jax.ShapeDtypeStruct((1, 1, rows, cols), BF16),
            jax.ShapeDtypeStruct(images.shape, BF16),
        ),
        in_specs=[vmem, vmem, vmem, vmem],
        out_specs=(hbm, hbm),
        scratch_shapes=[
            pltpu.VMEM((blocks, pieces, TILE, cols), BF16),
            dma((1 + blocks,)),
        ],
        compiler_params=pltpu.CompilerParams(vmem_limit_bytes=40 * 1024 * 1024),
        name="difference",
    )(*middle)


def solution(mesh):
    in_specs = (
        P("band", ("groups", "visit"), "strip", None),
        P("band", ("groups", "visit"), "strip", None),
        P("band", ("groups", "visit")),
        P(("groups", "visit"), None),
        P("groups"),
    )
    out_specs = (
        P("band", ("groups", "visit"), "strip", None),
        P("band", ("groups", "visit"), "strip", None),
    )
    step = functools.partial(body, mesh.shape["visit"], mesh.shape["strip"])
    return jax.shard_map(step, mesh=mesh, in_specs=in_specs, out_specs=out_specs, check_vma=False)
```

```python
import functools

import jax
import jax.numpy as jnp
import numpy as np
from jax import lax
from jax.experimental import pallas as pl
from jax.experimental.pallas import tpu as pltpu
from jax.sharding import PartitionSpec as P

BASES = 6
HALF = 9
TILE = 16

basis_rows = (0, 0, 1, 0, 2, 1)
basis_cols = (0, 1, 0, 2, 0, 1)
pairs = tuple((a, c) for a in range(BASES) for c in range(a, BASES))
MESH = pl.DeviceIdType.MESH
F32 = jnp.float32
BF16 = jnp.bfloat16


def kernel_taps():
    offsets = np.arange(2 * HALF + 1).astype(np.float32) - HALF
    gaussian = np.exp(-offsets * offsets / np.float32(18.0))
    centre = np.sum(offsets * offsets * gaussian * gaussian) / np.sum(gaussian * gaussian)
    table = np.stack([gaussian, offsets * gaussian, (offsets * offsets - centre) * gaussian])
    table = table / np.sqrt(np.sum(table * table, axis=1, keepdims=True))
    return table.astype(BF16).astype(np.float32)


def band_matrix(table, lead, trail, displace):
    index = np.arange(trail)[None, :] - np.arange(lead)[:, None] + displace
    inside = (index >= 0) & (index <= 2 * HALF)
    return np.where(inside[None], table[:, np.clip(index, 0, 2 * HALF)], 0.0)


def gather_matrix():
    result = np.zeros((BASES * 8, (len(pairs) + BASES) * TILE), np.float32)
    for n, (a, c) in enumerate(pairs):
        result[a * 8 + c, n * TILE : (n + 1) * TILE] = 1.0
        result[c * 8 + a, n * TILE : (n + 1) * TILE] = 1.0
    for a in range(BASES):
        n = len(pairs) + a
        result[a * 8 + 6, n * TILE : (n + 1) * TILE] = 1.0
    return result


def iota(shape, dim):
    return lax.broadcasted_iota(jnp.int32, shape, dim)


def nn(a, b):
    return jnp.dot(a, b, preferred_element_type=F32)


def nt(a, b, precision=None):
    return lax.dot_general(
        a, b, (((1,), (1,)), ((), ())), preferred_element_type=F32, precision=precision
    )


def kernel(
    visits, strips, distinct,
    images, masks, weight, cross, owner, cross_scalar, table_in,
    coadd_out, image_v, basis, mixers,
    mask_v, tables, use, use_image, send, recv, ids_own, ids, gath,
    prods, small, small_in,
    in_sem, const_sem, rs_send, rs_recv, id_send, id_recv, ag_send, ag_recv,
    halo_send, halo_recv,
    st_send, st_recv,
):
    pieces, rows, cols = images.shape[1:]
    blocks = rows // TILE
    span = pieces * TILE
    order = [0] + ([blocks - 1] if blocks > 1 else []) + list(range(1, blocks - 1))
    me = lax.axis_index("visit")
    strip = lax.axis_index("strip")

    loads = {}
    for t in order:
        piece_rows = pl.ds(t * TILE, TILE)
        loads[t] = ((
            pltpu.make_async_copy(masks.at[0, :, piece_rows, :], mask_v.at[t], in_sem.at[0, t]),
            pltpu.make_async_copy(images.at[0, :, piece_rows, :], image_v.at[t], in_sem.at[1, t]),
        ))
    constants = [pltpu.make_async_copy(table_in, tables, const_sem)]
    for t in order:
        for copy in loads[t]:
            copy.start()
    for copy in constants:
        copy.start()

    barrier = pltpu.get_barrier_semaphore()
    above = strip > 0
    below = strip < strips - 1

    def other_visit(k):
        return lax.rem(me + k, visits)

    for k in range(visits):
        for hop in range(strips):
            if k == 0 and hop == 0:
                continue
            target = {"visit": other_visit(k), "strip": lax.rem(strip + hop, strips)}
            pl.semaphore_signal(barrier, inc=1, device_id=target, device_id_type=MESH)

    seats = [owner[cross_scalar[0, j]] for j in range(pieces)]
    slots = [jnp.int32(0)] * distinct
    rank = jnp.int32(0)
    for q in range(visits):
        present = jnp.int32(0)
        for j in range(pieces):
            present = present | jnp.where(seats[j] == q, 1, 0)
        for d in range(distinct):
            slots[d] = slots[d] + jnp.where((present == 1) & (rank == d), q, 0)
        rank = rank + present

    position = jnp.zeros((1, pieces), jnp.int32)
    for p in range(visits):
        position = position + jnp.where(cross[...] == p, owner[p], 0)
    one_hot = (position == iota((128, pieces), 0)).astype(F32).astype(BF16)
    eq = jnp.concatenate([iota((TILE, 128), 1) == slots[d] for d in range(distinct)], axis=0)
    spread = nn(eq.astype(F32).astype(BF16), one_hot)
    spread = (spread * weight[...].astype(F32)).astype(BF16)
    e2 = iota((pieces, span), 0) == jnp.right_shift(iota((pieces, span), 1), 4)
    wide = nn(spread, e2.astype(F32).astype(BF16))
    same = (iota((distinct * TILE, span), 0) & (TILE - 1)) == (
        iota((distinct * TILE, span), 1) & (TILE - 1)
    )
    adder = jnp.where(same, wide, 0.0).astype(BF16)
    e_rows = jnp.right_shift(iota((span, 128), 0), 4) == iota((span, 128), 1)
    e_rows = e_rows.astype(F32).astype(BF16)
    row_hot = nt(e_rows[:, :pieces], one_hot)

    for t in order:
        for copy in loads[t]:
            copy.wait()
        usable = ((mask_v[t].reshape(span, cols) & 3) != 3).astype(F32).astype(BF16)
        masked = usable * image_v[t].reshape(span, cols)
        lanes = pl.ds(t * cols, cols)
        use[:, lanes] = usable
        use_image[:, lanes] = masked
        for part, value in enumerate((masked, usable)):
            total = nn(adder, value)
            for d in range(distinct):
                send[t, d, part] = total[d * TILE : (d + 1) * TILE].astype(BF16)
    names = jnp.zeros((1, 128), jnp.int32)
    for d in range(distinct):
        names = names + jnp.where(iota((1, 128), 1) == d, slots[d], 0)
    ids_own[...] = names.astype(F32)

    pl.semaphore_wait(barrier, visits * strips - 1)

    def block_of(r):
        return r ^ 1 if blocks % 2 == 0 else r

    my_block = me + 1 - 2 * lax.rem(me, 2) if blocks % 2 == 0 else me

    def reduce_copies(r, source):
        return (
            pltpu.make_async_remote_copy(
                src_ref=ids_own, dst_ref=ids.at[source],
                send_sem=id_send.at[r], recv_sem=id_recv.at[source],
                device_id={"visit": r}, device_id_type=MESH,
            ),
            pltpu.make_async_remote_copy(
                src_ref=send.at[block_of(r)], dst_ref=recv.at[source],
                send_sem=rs_send.at[r], recv_sem=rs_recv.at[source],
                device_id={"visit": r}, device_id_type=MESH,
            ),
        )

    def gather_copy(v, block):
        return pltpu.make_async_remote_copy(
            src_ref=gath.at[1 + block], dst_ref=gath.at[1 + block],
            send_sem=ag_send.at[v], recv_sem=ag_recv.at[block],
            device_id={"visit": v}, device_id_type=MESH,
        )

    for r in range(blocks):
        @pl.when(me != r)
        def _():
            for copy in reduce_copies(r, me):
                copy.start()

    @pl.when(jnp.logical_not(above))
    def _():
        gath[0] = jnp.zeros((visits, TILE, cols), BF16)

    @pl.when(jnp.logical_not(below))
    def _():
        gath[blocks + 1] = jnp.zeros((visits, TILE, cols), BF16)

    def reduce():
        recv[me] = send[my_block]
        ids[me] = ids_own[...]
        for v in range(visits):
            @pl.when(me != v)
            def _():
                for copy in reduce_copies(0, v):
                    copy.wait_recv()

        def one_patch(q, carry):
            numerator = jnp.zeros((TILE, cols), F32)
            denominator = jnp.zeros((TILE, cols), F32)
            number = lax.convert_element_type(q, F32)
            for v in range(visits):
                for d in range(distinct):
                    here = jnp.broadcast_to(ids[v][:, d : d + 1] == number, (TILE, cols))
                    numerator += jnp.where(here, recv[v, d, 0].astype(F32), 0.0)
                    denominator += jnp.where(here, recv[v, d, 1].astype(F32), 0.0)
            gath[1 + my_block, q] = (numerator / jnp.maximum(denominator, 1.0)).astype(BF16)
            return carry

        if visits <= 4:
            for q in range(visits):
                one_patch(q, 0)
        else:
            lax.fori_loop(0, visits, one_patch, 0)
        for v in range(visits):
            @pl.when(me != v)
            def _():
                gather_copy(v, my_block).start()

    if visits > blocks:
        pl.when(me < blocks)(reduce)
    else:
        reduce()

    for copy in constants:
        copy.wait()

    down = pltpu.make_async_remote_copy(
        src_ref=gath.at[blocks], dst_ref=gath.at[0],
        send_sem=halo_send.at[0], recv_sem=halo_recv.at[0],
        device_id={"strip": lax.rem(strip + 1, strips)}, device_id_type=MESH,
    )
    up = pltpu.make_async_remote_copy(
        src_ref=gath.at[1], dst_ref=gath.at[blocks + 1],
        send_sem=halo_send.at[1], recv_sem=halo_recv.at[1],
        device_id={"strip": lax.rem(strip + strips - 1, strips)}, device_id_type=MESH,
    )
    for t in [0, blocks - 1] + list(range(1, blocks - 1)):
        r = block_of(t)

        @pl.when(me != r)
        def _():
            gather_copy(r, t).wait_recv()

        if t == 0:
            pl.when(above)(up.start)
        if t == blocks - 1:
            pl.when(below)(down.start)
    pl.when(above)(down.wait_recv)
    pl.when(below)(up.wait_recv)
    for t in range(blocks):
        coadd_out[pl.ds(t * TILE, TILE), :] = gath[1 + t, me]

    top = BASES // 2 * cols
    vertical = tables[pl.ds(top, 3 * rows), pl.ds(0, rows + 2 * TILE)]
    top = top + 3 * rows

    def across(c):
        return tables[pl.ds(c * cols, cols), pl.ds(0, cols)]

    for d in range(distinct):
        template = jnp.concatenate([gath[i, slots[d]] for i in range(blocks + 2)], axis=0)
        smooth = nn(vertical, template).astype(BF16)
        planes = [None] * BASES
        for c in range(3):
            taken = [a for a in range(BASES) if basis_cols[a] == c]
            product = nn(smooth[: len(taken) * rows], across(c)).astype(BF16)
            for a in taken:
                r = basis_rows[a]
                planes[a] = product[r * rows : (r + 1) * rows]
        for a in range(BASES):
            for t in range(blocks):
                basis[d, pl.ds(a * TILE, TILE), pl.ds(t * cols, cols)] = planes[a][
                    t * TILE : (t + 1) * TILE
                ]
        for n, (a, c) in enumerate(pairs):
            product = planes[a] * planes[c]
            for t in range(blocks):
                prods[d, pl.ds(n * TILE, TILE), pl.ds(t * cols, cols)] = product[
                    t * TILE : (t + 1) * TILE
                ]

    def member(d):
        chosen = jnp.where(iota((span, 128), 1) == slots[d], row_hot, 0.0)
        return jnp.sum(chosen, axis=1, keepdims=True)

    def summed(values):
        return jnp.sum(values.reshape(pieces, TILE, values.shape[1]), axis=1)

    def keep(width):
        return (iota((span, width), 0) & (TILE - 1)) == (iota((span, width), 1) & (TILE - 1))

    wide_n = len(pairs) * TILE
    wide_b = BASES * TILE
    normal = jnp.zeros((pieces, wide_n), F32)
    right = jnp.zeros((pieces, wide_b), F32)
    for d in range(distinct):
        mine = member(d)
        normal = normal + summed(jnp.where(keep(wide_n), nt(use[...], prods[d]), 0.0) * mine)
        right = right + summed(jnp.where(keep(wide_b), nt(use_image[...], basis[d]), 0.0) * mine)
    normal_rows = tables[pl.ds(top, BASES * 8), pl.ds(0, wide_n)].astype(F32)
    right_rows = tables[pl.ds(top, BASES * 8), pl.ds(wide_n, wide_b)].astype(F32)
    system = nt(normal_rows, normal, lax.Precision.HIGHEST) + nt(
        right_rows, right, lax.Precision.HIGHEST
    )
    small[...] = jnp.concatenate(
        [system, jnp.zeros((BASES * 8, 128 - pieces), F32)], axis=1
    )
    exchanges = []
    for hop in range(1, strips):
        exchanges.append(pltpu.make_async_remote_copy(
            src_ref=small, dst_ref=small_in.at[hop - 1],
            send_sem=st_send.at[hop - 1], recv_sem=st_recv.at[hop - 1],
            device_id={"strip": lax.rem(strip + hop, strips)}, device_id_type=MESH,
        ))
    for copy in exchanges:
        copy.start()
    full = small[...]
    for hop in range(1, strips):
        exchanges[hop - 1].wait_recv()
        full = full + small_in[hop - 1]

    line = iota((8, 128), 0)
    table = [
        full[a * 8 : (a + 1) * 8] + jnp.where(line == a, 1.0, 0.0) for a in range(BASES)
    ]
    for column in range(BASES):
        pivot = table[column] / table[column][column : column + 1]
        for i in range(BASES):
            if i != column:
                table[i] = table[i] - table[i][column : column + 1] * pivot
        table[column] = pivot
    found = jnp.zeros((8, 128), F32)
    for a in range(BASES):
        found = found + jnp.where(line == a, table[a][BASES : BASES + 1], 0.0)
    high = found.astype(BF16).astype(F32)
    low = found - high
    both = jnp.concatenate([high, low], axis=0).astype(BF16)
    by_row = nt(e_rows, both).astype(BF16)
    wide_c = 2 * wide_b
    column = iota((16, wide_c), 1)
    source = jnp.where(
        column < wide_b, jnp.right_shift(column, 4), jnp.right_shift(column - wide_b, 4) + 8
    )
    e3 = (source == iota((16, wide_c), 0)).astype(F32).astype(BF16)
    mixer = jnp.where(keep(wide_c), nn(by_row, e3), 0.0)
    for d in range(distinct):
        mixers[d] = (mixer * member(d)).astype(BF16)

    for copy in exchanges:
        copy.wait_send()
    for r in range(blocks):
        @pl.when(me != r)
        def _():
            for copy in reduce_copies(r, me):
                copy.wait_send()

    def gathered():
        for v in range(visits):
            @pl.when(me != v)
            def _():
                gather_copy(v, my_block).wait_send()

    if visits > blocks:
        pl.when(me < blocks)(gathered)
    else:
        gathered()
    pl.when(below)(down.wait_send)
    pl.when(above)(up.wait_send)


def finish(coadd_in, image_v, basis, mixers, coadd_out, diff_out, diff_v, out_sem):
    distinct = basis.shape[0]
    blocks, pieces, _, cols = image_v.shape
    span = pieces * TILE
    stores = [pltpu.make_async_copy(coadd_in, coadd_out.at[0, 0], out_sem.at[0])]
    stores[0].start()
    for t in range(blocks):
        lanes = pl.ds(t * cols, cols)
        fitted = jnp.zeros((span, cols), F32)
        for d in range(distinct):
            planes = basis[d, :, lanes]
            fitted = fitted + nn(mixers[d], jnp.concatenate([planes, planes], axis=0))
        result = (image_v[t].reshape(span, cols).astype(F32) - fitted).astype(BF16)
        diff_v[t] = result.reshape(pieces, TILE, cols)
        copy = pltpu.make_async_copy(
            diff_v.at[t], diff_out.at[0, :, pl.ds(t * TILE, TILE), :], out_sem.at[1 + t]
        )
        copy.start()
        stores.append(copy)
    for copy in stores:
        copy.wait()


def body(visits, strips, images, mask_bits, visit_weight, intersection, patch_owner):
    _, pieces, rows, cols = images.shape
    blocks = rows // TILE
    distinct = max(1, patch_owner.shape[0] // 2)
    span = pieces * TILE
    taps = kernel_taps()
    collect = gather_matrix()
    width = max(collect.shape[1], cols, rows + 2 * TILE)
    width = -(-width // 128) * 128
    tables = jnp.asarray(np.concatenate([
        np.pad(part, ((0, 0), (0, width - part.shape[1])))
        for part in (
            np.transpose(band_matrix(taps, cols, cols, HALF), (0, 2, 1)).reshape(3 * cols, cols),
            band_matrix(taps, rows, rows + 2 * TILE, HALF - TILE).reshape(3 * rows, -1),
            collect,
        )
    ]), BF16)
    hbm = pl.BlockSpec(memory_space=pltpu.HBM)
    vmem = pl.BlockSpec(memory_space=pltpu.VMEM)
    smem = pl.BlockSpec(memory_space=pltpu.SMEM)
    dma = pltpu.SemaphoreType.DMA
    cross = intersection.reshape(1, pieces)
    middle = pl.pallas_call(
        functools.partial(kernel, visits, strips, distinct),
        out_shape=(
            jax.ShapeDtypeStruct((rows, cols), BF16),
            jax.ShapeDtypeStruct((blocks, pieces, TILE, cols), BF16),
            jax.ShapeDtypeStruct((distinct, BASES * TILE, blocks * cols), BF16),
            jax.ShapeDtypeStruct((distinct, span, 2 * BASES * TILE), BF16),
        ),
        in_specs=[hbm, hbm, vmem, vmem, smem, smem, hbm],
        out_specs=(vmem, vmem, vmem, vmem),
        scratch_shapes=[
            pltpu.VMEM((blocks, pieces, TILE, cols), jnp.int32),
            pltpu.VMEM(tables.shape, BF16),
            pltpu.VMEM((span, blocks * cols), BF16),
            pltpu.VMEM((span, blocks * cols), BF16),
            pltpu.VMEM((blocks, distinct, 2, TILE, cols), BF16),
            pltpu.VMEM((visits, distinct, 2, TILE, cols), BF16),
            pltpu.VMEM((1, 128), F32),
            pltpu.VMEM((visits, 1, 128), F32),
            pltpu.VMEM((blocks + 2, visits, TILE, cols), BF16),
            pltpu.VMEM((distinct, len(pairs) * TILE, blocks * cols), BF16),
            pltpu.VMEM((BASES * 8, 128), F32),
            pltpu.VMEM((max(1, strips - 1), BASES * 8, 128), F32),
            dma((2, blocks)),
            dma,
            dma((blocks,)),
            dma((visits,)),
            dma((blocks,)),
            dma((visits,)),
            dma((visits,)),
            dma((blocks,)),
            dma((2,)),
            dma((2,)),
            dma((max(1, strips - 1),)),
            dma((max(1, strips - 1),)),
        ],
        compiler_params=pltpu.CompilerParams(
            collective_id=0, has_side_effects=True, vmem_limit_bytes=55_100_000
        ),
        name="coadd_solve",
    )(
        images, mask_bits, visit_weight, cross, patch_owner, cross,
        tables,
    )
    return pl.pallas_call(
        finish,
        out_shape=(
            jax.ShapeDtypeStruct((1, 1, rows, cols), BF16),
            jax.ShapeDtypeStruct(images.shape, BF16),
        ),
        in_specs=[vmem, vmem, vmem, vmem],
        out_specs=(hbm, hbm),
        scratch_shapes=[
            pltpu.VMEM((blocks, pieces, TILE, cols), BF16),
            dma((1 + blocks,)),
        ],
        compiler_params=pltpu.CompilerParams(vmem_limit_bytes=40 * 1024 * 1024),
        name="difference",
    )(*middle)


def solution(mesh):
    in_specs = (
        P("band", ("groups", "visit"), "strip", None),
        P("band", ("groups", "visit"), "strip", None),
        P("band", ("groups", "visit")),
        P(("groups", "visit"), None),
        P("groups"),
    )
    out_specs = (
        P("band", ("groups", "visit"), "strip", None),
        P("band", ("groups", "visit"), "strip", None),
    )
    step = functools.partial(body, mesh.shape["visit"], mesh.shape["strip"])
    return jax.shard_map(step, mesh=mesh, in_specs=in_specs, out_specs=out_specs, check_vma=False)
```

```python
import functools

import jax
import jax.numpy as jnp
import numpy as np
from jax import lax
from jax.experimental import pallas as pl
from jax.experimental.pallas import tpu as pltpu
from jax.sharding import PartitionSpec as P

BASES = 6
HALF = 9
TILE = 16

basis_rows = (0, 0, 1, 0, 2, 1)
basis_cols = (0, 1, 0, 2, 0, 1)
pairs = tuple((a, c) for a in range(BASES) for c in range(a, BASES))
MESH = pl.DeviceIdType.MESH
F32 = jnp.float32
BF16 = jnp.bfloat16


def kernel_taps():
    offsets = np.arange(2 * HALF + 1).astype(np.float32) - HALF
    gaussian = np.exp(-offsets * offsets / np.float32(18.0))
    centre = np.sum(offsets * offsets * gaussian * gaussian) / np.sum(gaussian * gaussian)
    table = np.stack([gaussian, offsets * gaussian, (offsets * offsets - centre) * gaussian])
    table = table / np.sqrt(np.sum(table * table, axis=1, keepdims=True))
    return table.astype(BF16).astype(np.float32)


def band_matrix(table, lead, trail, displace):
    index = np.arange(trail)[None, :] - np.arange(lead)[:, None] + displace
    inside = (index >= 0) & (index <= 2 * HALF)
    return np.where(inside[None], table[:, np.clip(index, 0, 2 * HALF)], 0.0)


def gather_matrix():
    result = np.zeros((BASES * 8, (len(pairs) + BASES) * TILE), np.float32)
    for n, (a, c) in enumerate(pairs):
        result[a * 8 + c, n * TILE : (n + 1) * TILE] = 1.0
        result[c * 8 + a, n * TILE : (n + 1) * TILE] = 1.0
    for a in range(BASES):
        n = len(pairs) + a
        result[a * 8 + 6, n * TILE : (n + 1) * TILE] = 1.0
    return result


def iota(shape, dim):
    return lax.broadcasted_iota(jnp.int32, shape, dim)


def nn(a, b):
    return jnp.dot(a, b, preferred_element_type=F32)


def nt(a, b, precision=None):
    return lax.dot_general(
        a, b, (((1,), (1,)), ((), ())), preferred_element_type=F32, precision=precision
    )


def kernel(
    visits, strips, distinct,
    images, masks, weight, cross, owner, cross_scalar, table_in,
    coadd_out, image_v, basis, mixers,
    mask_v, tables, use, use_image, send, recv, ids_own, ids, gath,
    prods, small, small_in,
    in_sem, const_sem, rs_send, rs_recv, id_send, id_recv, ag_send, ag_recv,
    halo_send, halo_recv,
    st_send, st_recv,
):
    pieces, rows, cols = images.shape[1:]
    blocks = rows // TILE
    span = pieces * TILE
    halves = send.shape[0]
    lane = cols // halves
    order = [0] + ([blocks - 1] if blocks > 1 else []) + list(range(1, blocks - 1))
    me = lax.axis_index("visit")
    strip = lax.axis_index("strip")

    loads = {}
    for t in order:
        piece_rows = pl.ds(t * TILE, TILE)
        loads[t] = ((
            pltpu.make_async_copy(masks.at[0, :, piece_rows, :], mask_v.at[t], in_sem.at[0, t]),
            pltpu.make_async_copy(images.at[0, :, piece_rows, :], image_v.at[t], in_sem.at[1, t]),
        ))
    constants = [pltpu.make_async_copy(table_in, tables, const_sem)]
    for t in order:
        for copy in loads[t]:
            copy.start()
    for copy in constants:
        copy.start()

    barrier = pltpu.get_barrier_semaphore()
    above = strip > 0
    below = strip < strips - 1

    def other_visit(k):
        return lax.rem(me + k, visits)

    for k in range(visits):
        for hop in range(strips):
            if k == 0 and hop == 0:
                continue
            target = {"visit": other_visit(k), "strip": lax.rem(strip + hop, strips)}
            pl.semaphore_signal(barrier, inc=1, device_id=target, device_id_type=MESH)

    seats = [owner[cross_scalar[0, j]] for j in range(pieces)]
    slots = [jnp.int32(0)] * distinct
    rank = jnp.int32(0)
    for q in range(visits):
        present = jnp.int32(0)
        for j in range(pieces):
            present = present | jnp.where(seats[j] == q, 1, 0)
        for d in range(distinct):
            slots[d] = slots[d] + jnp.where((present == 1) & (rank == d), q, 0)
        rank = rank + present

    position = jnp.zeros((1, pieces), jnp.int32)
    for p in range(visits):
        position = position + jnp.where(cross[...] == p, owner[p], 0)
    one_hot = (position == iota((128, pieces), 0)).astype(F32).astype(BF16)
    eq = jnp.concatenate([iota((TILE, 128), 1) == slots[d] for d in range(distinct)], axis=0)
    spread = nn(eq.astype(F32).astype(BF16), one_hot)
    spread = (spread * weight[...].astype(F32)).astype(BF16)
    e2 = iota((pieces, span), 0) == jnp.right_shift(iota((pieces, span), 1), 4)
    wide = nn(spread, e2.astype(F32).astype(BF16))
    same = (iota((distinct * TILE, span), 0) & (TILE - 1)) == (
        iota((distinct * TILE, span), 1) & (TILE - 1)
    )
    adder = jnp.where(same, wide, 0.0).astype(BF16)
    e_rows = jnp.right_shift(iota((span, 128), 0), 4) == iota((span, 128), 1)
    e_rows = e_rows.astype(F32).astype(BF16)
    row_hot = nt(e_rows[:, :pieces], one_hot)

    for t in order:
        for copy in loads[t]:
            copy.wait()
        usable = ((mask_v[t].reshape(span, cols) & 3) != 3).astype(F32).astype(BF16)
        masked = usable * image_v[t].reshape(span, cols)
        lanes = pl.ds(t * cols, cols)
        use[:, lanes] = usable
        use_image[:, lanes] = masked
        for part, value in enumerate((masked, usable)):
            total = nn(adder, value)
            for d in range(distinct):
                block = total[d * TILE : (d + 1) * TILE].astype(BF16)
                for h in range(halves):
                    send[h, t, d, part] = block[:, h * lane : (h + 1) * lane]
    names = jnp.zeros((1, 128), jnp.int32)
    for d in range(distinct):
        names = names + jnp.where(iota((1, 128), 1) == d, slots[d], 0)
    ids_own[...] = names.astype(F32)

    pl.semaphore_wait(barrier, visits * strips - 1)

    def block_of(r):
        return r ^ 1 if blocks % 2 == 0 else r

    my_block = me + 1 - 2 * lax.rem(me, 2) if blocks % 2 == 0 else me

    def reduce_copies(h, r, source):
        sums_copy = pltpu.make_async_remote_copy(
            src_ref=send.at[h, block_of(r)], dst_ref=recv.at[h, source],
            send_sem=rs_send.at[h, r], recv_sem=rs_recv.at[h, source],
            device_id={"visit": r}, device_id_type=MESH,
        )
        if h > 0:
            return (sums_copy,)
        names_copy = pltpu.make_async_remote_copy(
            src_ref=ids_own, dst_ref=ids.at[source],
            send_sem=id_send.at[r], recv_sem=id_recv.at[source],
            device_id={"visit": r}, device_id_type=MESH,
        )
        return (names_copy, sums_copy)

    def gather_copy(h, v, block):
        return pltpu.make_async_remote_copy(
            src_ref=gath.at[h, 1 + block], dst_ref=gath.at[h, 1 + block],
            send_sem=ag_send.at[h, v], recv_sem=ag_recv.at[h, block],
            device_id={"visit": v}, device_id_type=MESH,
        )

    for h in range(halves):
        for r in range(blocks):
            @pl.when(me != r)
            def _():
                for copy in reduce_copies(h, r, me):
                    copy.start()

    @pl.when(jnp.logical_not(above))
    def _():
        gath[:, 0] = jnp.zeros((halves, visits, TILE, lane), BF16)

    @pl.when(jnp.logical_not(below))
    def _():
        gath[:, blocks + 1] = jnp.zeros((halves, visits, TILE, lane), BF16)

    def reduce(h):
        recv[h, me] = send[h, my_block]
        if h == 0:
            ids[me] = ids_own[...]
        for v in range(visits):
            @pl.when(me != v)
            def _():
                for copy in reduce_copies(h, 0, v):
                    copy.wait_recv()

        def one_patch(q, carry):
            numerator = jnp.zeros((TILE, lane), F32)
            denominator = jnp.zeros((TILE, lane), F32)
            number = lax.convert_element_type(q, F32)
            for v in range(visits):
                for d in range(distinct):
                    here = jnp.broadcast_to(ids[v][:, d : d + 1] == number, (TILE, lane))
                    numerator += jnp.where(here, recv[h, v, d, 0].astype(F32), 0.0)
                    denominator += jnp.where(here, recv[h, v, d, 1].astype(F32), 0.0)
            gath[h, 1 + my_block, q] = (numerator / jnp.maximum(denominator, 1.0)).astype(BF16)
            return carry

        if visits <= 4:
            for q in range(visits):
                one_patch(q, 0)
        else:
            lax.fori_loop(0, visits, one_patch, 0)
        for v in range(visits):
            @pl.when(me != v)
            def _():
                gather_copy(h, v, my_block).start()

    for h in range(halves):
        if visits > blocks:
            pl.when(me < blocks)(functools.partial(reduce, h))
        else:
            reduce(h)

    for copy in constants:
        copy.wait()

    downs = [pltpu.make_async_remote_copy(
        src_ref=gath.at[h, blocks], dst_ref=gath.at[h, 0],
        send_sem=halo_send.at[h, 0], recv_sem=halo_recv.at[h, 0],
        device_id={"strip": lax.rem(strip + 1, strips)}, device_id_type=MESH,
    ) for h in range(halves)]
    ups = [pltpu.make_async_remote_copy(
        src_ref=gath.at[h, 1], dst_ref=gath.at[h, blocks + 1],
        send_sem=halo_send.at[h, 1], recv_sem=halo_recv.at[h, 1],
        device_id={"strip": lax.rem(strip + strips - 1, strips)}, device_id_type=MESH,
    ) for h in range(halves)]
    edges = sorted({0, blocks - 1})
    inner = list(range(1, blocks - 1))
    for h, t in [(h, t) for part in (edges, inner) for h in range(halves) for t in part]:
        r = block_of(t)

        @pl.when(me != r)
        def _():
            gather_copy(h, r, t).wait_recv()

        if t == 0:
            pl.when(above)(ups[h].start)
        if t == blocks - 1:
            pl.when(below)(downs[h].start)
    for h in range(halves):
        pl.when(above)(downs[h].wait_recv)
        pl.when(below)(ups[h].wait_recv)
    for h in range(halves):
        for t in range(blocks):
            coadd_out[pl.ds(t * TILE, TILE), pl.ds(h * lane, lane)] = gath[h, 1 + t, me]

    top = BASES // 2 * cols
    vertical = tables[pl.ds(top, 3 * rows), pl.ds(0, rows + 2 * TILE)]
    top = top + 3 * rows

    def across(c):
        return tables[pl.ds(c * cols, cols), pl.ds(0, cols)]

    for d in range(distinct):
        template = jnp.concatenate([
            jnp.concatenate([gath[h, i, slots[d]] for i in range(blocks + 2)], axis=0)
            for h in range(halves)
        ], axis=1)
        smooth = nn(vertical, template).astype(BF16)
        planes = [None] * BASES
        for c in range(3):
            taken = [a for a in range(BASES) if basis_cols[a] == c]
            product = nn(smooth[: len(taken) * rows], across(c)).astype(BF16)
            for a in taken:
                r = basis_rows[a]
                planes[a] = product[r * rows : (r + 1) * rows]
        for a in range(BASES):
            for t in range(blocks):
                basis[d, pl.ds(a * TILE, TILE), pl.ds(t * cols, cols)] = planes[a][
                    t * TILE : (t + 1) * TILE
                ]
        for n, (a, c) in enumerate(pairs):
            product = planes[a] * planes[c]
            for t in range(blocks):
                prods[d, pl.ds(n * TILE, TILE), pl.ds(t * cols, cols)] = product[
                    t * TILE : (t + 1) * TILE
                ]

    def member(d):
        chosen = jnp.where(iota((span, 128), 1) == slots[d], row_hot, 0.0)
        return jnp.sum(chosen, axis=1, keepdims=True)

    def summed(values):
        return jnp.sum(values.reshape(pieces, TILE, values.shape[1]), axis=1)

    def keep(width):
        return (iota((span, width), 0) & (TILE - 1)) == (iota((span, width), 1) & (TILE - 1))

    wide_n = len(pairs) * TILE
    wide_b = BASES * TILE
    normal = jnp.zeros((pieces, wide_n), F32)
    right = jnp.zeros((pieces, wide_b), F32)
    for d in range(distinct):
        mine = member(d)
        normal = normal + summed(jnp.where(keep(wide_n), nt(use[...], prods[d]), 0.0) * mine)
        right = right + summed(jnp.where(keep(wide_b), nt(use_image[...], basis[d]), 0.0) * mine)
    normal_rows = tables[pl.ds(top, BASES * 8), pl.ds(0, wide_n)].astype(F32)
    right_rows = tables[pl.ds(top, BASES * 8), pl.ds(wide_n, wide_b)].astype(F32)
    system = nt(normal_rows, normal, lax.Precision.HIGHEST) + nt(
        right_rows, right, lax.Precision.HIGHEST
    )
    small[...] = jnp.concatenate(
        [system, jnp.zeros((BASES * 8, 128 - pieces), F32)], axis=1
    )
    exchanges = []
    for hop in range(1, strips):
        exchanges.append(pltpu.make_async_remote_copy(
            src_ref=small, dst_ref=small_in.at[hop - 1],
            send_sem=st_send.at[hop - 1], recv_sem=st_recv.at[hop - 1],
            device_id={"strip": lax.rem(strip + hop, strips)}, device_id_type=MESH,
        ))
    for copy in exchanges:
        copy.start()
    full = small[...]
    for hop in range(1, strips):
        exchanges[hop - 1].wait_recv()
        full = full + small_in[hop - 1]

    line = iota((8, 128), 0)
    table = [
        full[a * 8 : (a + 1) * 8] + jnp.where(line == a, 1.0, 0.0) for a in range(BASES)
    ]
    for column in range(BASES):
        pivot = table[column] / table[column][column : column + 1]
        for i in range(BASES):
            if i != column:
                table[i] = table[i] - table[i][column : column + 1] * pivot
        table[column] = pivot
    found = jnp.zeros((8, 128), F32)
    for a in range(BASES):
        found = found + jnp.where(line == a, table[a][BASES : BASES + 1], 0.0)
    high = found.astype(BF16).astype(F32)
    low = found - high
    both = jnp.concatenate([high, low], axis=0).astype(BF16)
    by_row = nt(e_rows, both).astype(BF16)
    wide_c = 2 * wide_b
    column = iota((16, wide_c), 1)
    source = jnp.where(
        column < wide_b, jnp.right_shift(column, 4), jnp.right_shift(column - wide_b, 4) + 8
    )
    e3 = (source == iota((16, wide_c), 0)).astype(F32).astype(BF16)
    mixer = jnp.where(keep(wide_c), nn(by_row, e3), 0.0)
    for d in range(distinct):
        mixers[d] = (mixer * member(d)).astype(BF16)

    for copy in exchanges:
        copy.wait_send()
    def gathered(h):
        for v in range(visits):
            @pl.when(me != v)
            def _():
                gather_copy(h, v, my_block).wait_send()

    for h in range(halves):
        for r in range(blocks):
            @pl.when(me != r)
            def _():
                for copy in reduce_copies(h, r, me):
                    copy.wait_send()

        if visits > blocks:
            pl.when(me < blocks)(functools.partial(gathered, h))
        else:
            gathered(h)
        pl.when(below)(downs[h].wait_send)
        pl.when(above)(ups[h].wait_send)


def finish(coadd_in, image_v, basis, mixers, coadd_out, diff_out, diff_v, out_sem):
    distinct = basis.shape[0]
    blocks, pieces, _, cols = image_v.shape
    span = pieces * TILE
    stores = [pltpu.make_async_copy(coadd_in, coadd_out.at[0, 0], out_sem.at[0])]
    stores[0].start()
    for t in range(blocks):
        lanes = pl.ds(t * cols, cols)
        fitted = jnp.zeros((span, cols), F32)
        for d in range(distinct):
            planes = basis[d, :, lanes]
            fitted = fitted + nn(mixers[d], jnp.concatenate([planes, planes], axis=0))
        result = (image_v[t].reshape(span, cols).astype(F32) - fitted).astype(BF16)
        diff_v[t] = result.reshape(pieces, TILE, cols)
        copy = pltpu.make_async_copy(
            diff_v.at[t], diff_out.at[0, :, pl.ds(t * TILE, TILE), :], out_sem.at[1 + t]
        )
        copy.start()
        stores.append(copy)
    for copy in stores:
        copy.wait()


def body(visits, strips, images, mask_bits, visit_weight, intersection, patch_owner):
    _, pieces, rows, cols = images.shape
    blocks = rows // TILE
    distinct = max(1, patch_owner.shape[0] // 2)
    span = pieces * TILE
    halves = max(1, cols // 128)
    lane = cols // halves
    taps = kernel_taps()
    collect = gather_matrix()
    width = max(collect.shape[1], cols, rows + 2 * TILE)
    width = -(-width // 128) * 128
    tables = jnp.asarray(np.concatenate([
        np.pad(part, ((0, 0), (0, width - part.shape[1])))
        for part in (
            np.transpose(band_matrix(taps, cols, cols, HALF), (0, 2, 1)).reshape(3 * cols, cols),
            band_matrix(taps, rows, rows + 2 * TILE, HALF - TILE).reshape(3 * rows, -1),
            collect,
        )
    ]), BF16)
    hbm = pl.BlockSpec(memory_space=pltpu.HBM)
    vmem = pl.BlockSpec(memory_space=pltpu.VMEM)
    smem = pl.BlockSpec(memory_space=pltpu.SMEM)
    dma = pltpu.SemaphoreType.DMA
    cross = intersection.reshape(1, pieces)
    middle = pl.pallas_call(
        functools.partial(kernel, visits, strips, distinct),
        out_shape=(
            jax.ShapeDtypeStruct((rows, cols), BF16),
            jax.ShapeDtypeStruct((blocks, pieces, TILE, cols), BF16),
            jax.ShapeDtypeStruct((distinct, BASES * TILE, blocks * cols), BF16),
            jax.ShapeDtypeStruct((distinct, span, 2 * BASES * TILE), BF16),
        ),
        in_specs=[hbm, hbm, vmem, vmem, smem, smem, hbm],
        out_specs=(vmem, vmem, vmem, vmem),
        scratch_shapes=[
            pltpu.VMEM((blocks, pieces, TILE, cols), jnp.int32),
            pltpu.VMEM(tables.shape, BF16),
            pltpu.VMEM((span, blocks * cols), BF16),
            pltpu.VMEM((span, blocks * cols), BF16),
            pltpu.VMEM((halves, blocks, distinct, 2, TILE, lane), BF16),
            pltpu.VMEM((halves, visits, distinct, 2, TILE, lane), BF16),
            pltpu.VMEM((1, 128), F32),
            pltpu.VMEM((visits, 1, 128), F32),
            pltpu.VMEM((halves, blocks + 2, visits, TILE, lane), BF16),
            pltpu.VMEM((distinct, len(pairs) * TILE, blocks * cols), BF16),
            pltpu.VMEM((BASES * 8, 128), F32),
            pltpu.VMEM((max(1, strips - 1), BASES * 8, 128), F32),
            dma((2, blocks)),
            dma,
            dma((halves, blocks)),
            dma((halves, visits)),
            dma((blocks,)),
            dma((visits,)),
            dma((halves, visits)),
            dma((halves, blocks)),
            dma((halves, 2)),
            dma((halves, 2)),
            dma((max(1, strips - 1),)),
            dma((max(1, strips - 1),)),
        ],
        compiler_params=pltpu.CompilerParams(
            collective_id=0, has_side_effects=True, vmem_limit_bytes=55_100_000
        ),
        name="coadd_solve",
    )(
        images, mask_bits, visit_weight, cross, patch_owner, cross,
        tables,
    )
    return pl.pallas_call(
        finish,
        out_shape=(
            jax.ShapeDtypeStruct((1, 1, rows, cols), BF16),
            jax.ShapeDtypeStruct(images.shape, BF16),
        ),
        in_specs=[vmem, vmem, vmem, vmem],
        out_specs=(hbm, hbm),
        scratch_shapes=[
            pltpu.VMEM((blocks, pieces, TILE, cols), BF16),
            dma((1 + blocks,)),
        ],
        compiler_params=pltpu.CompilerParams(vmem_limit_bytes=40 * 1024 * 1024),
        name="difference",
    )(*middle)


def solution(mesh):
    in_specs = (
        P("band", ("groups", "visit"), "strip", None),
        P("band", ("groups", "visit"), "strip", None),
        P("band", ("groups", "visit")),
        P(("groups", "visit"), None),
        P("groups"),
    )
    out_specs = (
        P("band", ("groups", "visit"), "strip", None),
        P("band", ("groups", "visit"), "strip", None),
    )
    step = functools.partial(body, mesh.shape["visit"], mesh.shape["strip"])
    return jax.shard_map(step, mesh=mesh, in_specs=in_specs, out_specs=out_specs, check_vma=False)
```

```python
import functools

import jax
import jax.numpy as jnp
import numpy as np
from jax import lax
from jax.experimental import pallas as pl
from jax.experimental.pallas import tpu as pltpu
from jax.sharding import PartitionSpec as P

BASES = 6
HALF = 9
TILE = 16

basis_rows = (0, 0, 1, 0, 2, 1)
basis_cols = (0, 1, 0, 2, 0, 1)
pairs = tuple((a, c) for a in range(BASES) for c in range(a, BASES))
MESH = pl.DeviceIdType.MESH
F32 = jnp.float32
BF16 = jnp.bfloat16


def kernel_taps():
    offsets = np.arange(2 * HALF + 1).astype(np.float32) - HALF
    gaussian = np.exp(-offsets * offsets / np.float32(18.0))
    centre = np.sum(offsets * offsets * gaussian * gaussian) / np.sum(gaussian * gaussian)
    table = np.stack([gaussian, offsets * gaussian, (offsets * offsets - centre) * gaussian])
    table = table / np.sqrt(np.sum(table * table, axis=1, keepdims=True))
    return table.astype(BF16).astype(np.float32)


def band_matrix(table, lead, trail, displace):
    index = np.arange(trail)[None, :] - np.arange(lead)[:, None] + displace
    inside = (index >= 0) & (index <= 2 * HALF)
    return np.where(inside[None], table[:, np.clip(index, 0, 2 * HALF)], 0.0)


def gather_matrix():
    result = np.zeros((BASES * 8, (len(pairs) + BASES) * TILE), np.float32)
    for n, (a, c) in enumerate(pairs):
        result[a * 8 + c, n * TILE : (n + 1) * TILE] = 1.0
        result[c * 8 + a, n * TILE : (n + 1) * TILE] = 1.0
    for a in range(BASES):
        n = len(pairs) + a
        result[a * 8 + 6, n * TILE : (n + 1) * TILE] = 1.0
    return result


def iota(shape, dim):
    return lax.broadcasted_iota(jnp.int32, shape, dim)


def nn(a, b):
    return jnp.dot(a, b, preferred_element_type=F32)


def nt(a, b, precision=None):
    return lax.dot_general(
        a, b, (((1,), (1,)), ((), ())), preferred_element_type=F32, precision=precision
    )


def kernel(
    visits, strips, distinct,
    images, masks, weight, cross, owner, cross_scalar, table_in,
    coadd_out, image_v, basis, mixers,
    mask_v, tables, use, use_image, send, recv, ids_own, ids, gath,
    prods, small, small_in,
    in_sem, const_sem, rs_send, rs_recv, id_send, id_recv, ag_send, ag_recv,
    halo_send, halo_recv,
    st_send, st_recv,
):
    pieces, rows, cols = images.shape[1:]
    blocks = rows // TILE
    span = pieces * TILE
    order = [0] + ([blocks - 1] if blocks > 1 else []) + list(range(1, blocks - 1))
    me = lax.axis_index("visit")
    strip = lax.axis_index("strip")

    loads = {}
    for t in order:
        piece_rows = pl.ds(t * TILE, TILE)
        loads[t] = ((
            pltpu.make_async_copy(masks.at[0, :, piece_rows, :], mask_v.at[t], in_sem.at[0, t]),
            pltpu.make_async_copy(images.at[0, :, piece_rows, :], image_v.at[t], in_sem.at[1, t]),
        ))
    constants = [pltpu.make_async_copy(table_in, tables, const_sem)]
    for t in order:
        for copy in loads[t]:
            copy.start()
    for copy in constants:
        copy.start()

    barrier = pltpu.get_barrier_semaphore()
    above = strip > 0
    below = strip < strips - 1

    def other_visit(k):
        return lax.rem(me + k, visits)

    for k in range(visits):
        for hop in range(strips):
            if k == 0 and hop == 0:
                continue
            target = {"visit": other_visit(k), "strip": lax.rem(strip + hop, strips)}
            pl.semaphore_signal(barrier, inc=1, device_id=target, device_id_type=MESH)

    seats = [owner[cross_scalar[0, j]] for j in range(pieces)]
    slots = [jnp.int32(0)] * distinct
    rank = jnp.int32(0)
    for q in range(visits):
        present = jnp.int32(0)
        for j in range(pieces):
            present = present | jnp.where(seats[j] == q, 1, 0)
        for d in range(distinct):
            slots[d] = slots[d] + jnp.where((present == 1) & (rank == d), q, 0)
        rank = rank + present

    position = jnp.zeros((1, pieces), jnp.int32)
    for p in range(visits):
        position = position + jnp.where(cross[...] == p, owner[p], 0)
    one_hot = (position == iota((128, pieces), 0)).astype(F32).astype(BF16)
    eq = jnp.concatenate([iota((TILE, 128), 1) == slots[d] for d in range(distinct)], axis=0)
    spread = nn(eq.astype(F32).astype(BF16), one_hot)
    spread = (spread * weight[...].astype(F32)).astype(BF16)
    e2 = iota((pieces, span), 0) == jnp.right_shift(iota((pieces, span), 1), 4)
    wide = nn(spread, e2.astype(F32).astype(BF16))
    same = (iota((distinct * TILE, span), 0) & (TILE - 1)) == (
        iota((distinct * TILE, span), 1) & (TILE - 1)
    )
    adder = jnp.where(same, wide, 0.0).astype(BF16)
    e_rows = jnp.right_shift(iota((span, 128), 0), 4) == iota((span, 128), 1)
    e_rows = e_rows.astype(F32).astype(BF16)
    row_hot = nt(e_rows[:, :pieces], one_hot)

    for t in order:
        for copy in loads[t]:
            copy.wait()
        usable = ((mask_v[t].reshape(span, cols) & 3) != 3).astype(F32).astype(BF16)
        masked = usable * image_v[t].reshape(span, cols)
        lanes = pl.ds(t * cols, cols)
        use[:, lanes] = usable
        use_image[:, lanes] = masked
        for part, value in enumerate((masked, usable)):
            total = nn(adder, value)
            for d in range(distinct):
                send[t, d, part] = total[d * TILE : (d + 1) * TILE].astype(BF16)
    names = jnp.zeros((1, 128), jnp.int32)
    for d in range(distinct):
        names = names + jnp.where(iota((1, 128), 1) == d, slots[d], 0)
    ids_own[...] = names.astype(F32)

    pl.semaphore_wait(barrier, visits * strips - 1)

    def block_of(r):
        return r ^ 1 if blocks % 2 == 0 else r

    my_block = me + 1 - 2 * lax.rem(me, 2) if blocks % 2 == 0 else me

    def reduce_copies(r, source):
        return (
            pltpu.make_async_remote_copy(
                src_ref=ids_own, dst_ref=ids.at[source],
                send_sem=id_send.at[r], recv_sem=id_recv.at[source],
                device_id={"visit": r}, device_id_type=MESH,
            ),
            pltpu.make_async_remote_copy(
                src_ref=send.at[block_of(r)], dst_ref=recv.at[source],
                send_sem=rs_send.at[r], recv_sem=rs_recv.at[source],
                device_id={"visit": r}, device_id_type=MESH,
            ),
        )

    def gather_copy(v, block):
        return pltpu.make_async_remote_copy(
            src_ref=gath.at[1 + block], dst_ref=gath.at[1 + block],
            send_sem=ag_send.at[v], recv_sem=ag_recv.at[block],
            device_id={"visit": v}, device_id_type=MESH,
        )

    low = me * 2 < visits
    for side, targets in ((low, range(blocks - 1, -1, -1)), (jnp.logical_not(low), range(blocks))):
        for r in targets:
            @pl.when(jnp.logical_and(side, me != r))
            def _():
                for copy in reduce_copies(r, me):
                    copy.start()

    @pl.when(jnp.logical_not(above))
    def _():
        gath[0] = jnp.zeros((visits, TILE, cols), BF16)

    @pl.when(jnp.logical_not(below))
    def _():
        gath[blocks + 1] = jnp.zeros((visits, TILE, cols), BF16)

    def reduce():
        recv[me] = send[my_block]
        ids[me] = ids_own[...]
        for v in range(visits):
            @pl.when(me != v)
            def _():
                for copy in reduce_copies(0, v):
                    copy.wait_recv()

        def one_patch(q, carry):
            numerator = jnp.zeros((TILE, cols), F32)
            denominator = jnp.zeros((TILE, cols), F32)
            number = lax.convert_element_type(q, F32)
            for v in range(visits):
                for d in range(distinct):
                    here = jnp.broadcast_to(ids[v][:, d : d + 1] == number, (TILE, cols))
                    numerator += jnp.where(here, recv[v, d, 0].astype(F32), 0.0)
                    denominator += jnp.where(here, recv[v, d, 1].astype(F32), 0.0)
            gath[1 + my_block, q] = (numerator / jnp.maximum(denominator, 1.0)).astype(BF16)
            return carry

        if visits <= 4:
            for q in range(visits):
                one_patch(q, 0)
        else:
            lax.fori_loop(0, visits, one_patch, 0)
        for side, targets in (
            (low, range(visits - 1, -1, -1)), (jnp.logical_not(low), range(visits))
        ):
            for v in targets:
                @pl.when(jnp.logical_and(side, me != v))
                def _():
                    gather_copy(v, my_block).start()

    if visits > blocks:
        pl.when(me < blocks)(reduce)
    else:
        reduce()

    for copy in constants:
        copy.wait()

    down = pltpu.make_async_remote_copy(
        src_ref=gath.at[blocks], dst_ref=gath.at[0],
        send_sem=halo_send.at[0], recv_sem=halo_recv.at[0],
        device_id={"strip": lax.rem(strip + 1, strips)}, device_id_type=MESH,
    )
    up = pltpu.make_async_remote_copy(
        src_ref=gath.at[1], dst_ref=gath.at[blocks + 1],
        send_sem=halo_send.at[1], recv_sem=halo_recv.at[1],
        device_id={"strip": lax.rem(strip + strips - 1, strips)}, device_id_type=MESH,
    )
    for t in [0, blocks - 1] + list(range(1, blocks - 1)):
        r = block_of(t)

        @pl.when(me != r)
        def _():
            gather_copy(r, t).wait_recv()

        if t == 0:
            pl.when(above)(up.start)
        if t == blocks - 1:
            pl.when(below)(down.start)
    pl.when(above)(down.wait_recv)
    pl.when(below)(up.wait_recv)
    for t in range(blocks):
        coadd_out[pl.ds(t * TILE, TILE), :] = gath[1 + t, me]

    top = BASES // 2 * cols
    vertical = tables[pl.ds(top, 3 * rows), pl.ds(0, rows + 2 * TILE)]
    top = top + 3 * rows

    def across(c):
        return tables[pl.ds(c * cols, cols), pl.ds(0, cols)]

    for d in range(distinct):
        template = jnp.concatenate([gath[i, slots[d]] for i in range(blocks + 2)], axis=0)
        smooth = nn(vertical, template).astype(BF16)
        planes = [None] * BASES
        for c in range(3):
            taken = [a for a in range(BASES) if basis_cols[a] == c]
            product = nn(smooth[: len(taken) * rows], across(c)).astype(BF16)
            for a in taken:
                r = basis_rows[a]
                planes[a] = product[r * rows : (r + 1) * rows]
        for a in range(BASES):
            for t in range(blocks):
                basis[d, pl.ds(a * TILE, TILE), pl.ds(t * cols, cols)] = planes[a][
                    t * TILE : (t + 1) * TILE
                ]
        for n, (a, c) in enumerate(pairs):
            product = planes[a] * planes[c]
            for t in range(blocks):
                prods[d, pl.ds(n * TILE, TILE), pl.ds(t * cols, cols)] = product[
                    t * TILE : (t + 1) * TILE
                ]

    def member(d):
        chosen = jnp.where(iota((span, 128), 1) == slots[d], row_hot, 0.0)
        return jnp.sum(chosen, axis=1, keepdims=True)

    def summed(values):
        return jnp.sum(values.reshape(pieces, TILE, values.shape[1]), axis=1)

    def keep(width):
        return (iota((span, width), 0) & (TILE - 1)) == (iota((span, width), 1) & (TILE - 1))

    wide_n = len(pairs) * TILE
    wide_b = BASES * TILE
    normal = jnp.zeros((pieces, wide_n), F32)
    right = jnp.zeros((pieces, wide_b), F32)
    for d in range(distinct):
        mine = member(d)
        normal = normal + summed(jnp.where(keep(wide_n), nt(use[...], prods[d]), 0.0) * mine)
        right = right + summed(jnp.where(keep(wide_b), nt(use_image[...], basis[d]), 0.0) * mine)
    normal_rows = tables[pl.ds(top, BASES * 8), pl.ds(0, wide_n)].astype(F32)
    right_rows = tables[pl.ds(top, BASES * 8), pl.ds(wide_n, wide_b)].astype(F32)
    system = nt(normal_rows, normal, lax.Precision.HIGHEST) + nt(
        right_rows, right, lax.Precision.HIGHEST
    )
    small[...] = jnp.concatenate(
        [system, jnp.zeros((BASES * 8, 128 - pieces), F32)], axis=1
    )
    exchanges = []
    for hop in range(1, strips):
        exchanges.append(pltpu.make_async_remote_copy(
            src_ref=small, dst_ref=small_in.at[hop - 1],
            send_sem=st_send.at[hop - 1], recv_sem=st_recv.at[hop - 1],
            device_id={"strip": lax.rem(strip + hop, strips)}, device_id_type=MESH,
        ))
    for copy in exchanges:
        copy.start()
    full = small[...]
    for hop in range(1, strips):
        exchanges[hop - 1].wait_recv()
        full = full + small_in[hop - 1]

    line = iota((8, 128), 0)
    table = [
        full[a * 8 : (a + 1) * 8] + jnp.where(line == a, 1.0, 0.0) for a in range(BASES)
    ]
    for column in range(BASES):
        pivot = table[column] / table[column][column : column + 1]
        for i in range(BASES):
            if i != column:
                table[i] = table[i] - table[i][column : column + 1] * pivot
        table[column] = pivot
    found = jnp.zeros((8, 128), F32)
    for a in range(BASES):
        found = found + jnp.where(line == a, table[a][BASES : BASES + 1], 0.0)
    high = found.astype(BF16).astype(F32)
    low = found - high
    both = jnp.concatenate([high, low], axis=0).astype(BF16)
    by_row = nt(e_rows, both).astype(BF16)
    wide_c = 2 * wide_b
    column = iota((16, wide_c), 1)
    source = jnp.where(
        column < wide_b, jnp.right_shift(column, 4), jnp.right_shift(column - wide_b, 4) + 8
    )
    e3 = (source == iota((16, wide_c), 0)).astype(F32).astype(BF16)
    mixer = jnp.where(keep(wide_c), nn(by_row, e3), 0.0)
    for d in range(distinct):
        mixers[d] = (mixer * member(d)).astype(BF16)

    for copy in exchanges:
        copy.wait_send()
    for r in range(blocks):
        @pl.when(me != r)
        def _():
            for copy in reduce_copies(r, me):
                copy.wait_send()

    def gathered():
        for v in range(visits):
            @pl.when(me != v)
            def _():
                gather_copy(v, my_block).wait_send()

    if visits > blocks:
        pl.when(me < blocks)(gathered)
    else:
        gathered()
    pl.when(below)(down.wait_send)
    pl.when(above)(up.wait_send)


def finish(coadd_in, image_v, basis, mixers, coadd_out, diff_out, diff_v, out_sem):
    distinct = basis.shape[0]
    blocks, pieces, _, cols = image_v.shape
    span = pieces * TILE
    stores = [pltpu.make_async_copy(coadd_in, coadd_out.at[0, 0], out_sem.at[0])]
    stores[0].start()
    for t in range(blocks):
        lanes = pl.ds(t * cols, cols)
        fitted = jnp.zeros((span, cols), F32)
        for d in range(distinct):
            planes = basis[d, :, lanes]
            fitted = fitted + nn(mixers[d], jnp.concatenate([planes, planes], axis=0))
        result = (image_v[t].reshape(span, cols).astype(F32) - fitted).astype(BF16)
        diff_v[t] = result.reshape(pieces, TILE, cols)
        copy = pltpu.make_async_copy(
            diff_v.at[t], diff_out.at[0, :, pl.ds(t * TILE, TILE), :], out_sem.at[1 + t]
        )
        copy.start()
        stores.append(copy)
    for copy in stores:
        copy.wait()


def body(visits, strips, images, mask_bits, visit_weight, intersection, patch_owner):
    _, pieces, rows, cols = images.shape
    blocks = rows // TILE
    distinct = max(1, patch_owner.shape[0] // 2)
    span = pieces * TILE
    taps = kernel_taps()
    collect = gather_matrix()
    width = max(collect.shape[1], cols, rows + 2 * TILE)
    width = -(-width // 128) * 128
    tables = jnp.asarray(np.concatenate([
        np.pad(part, ((0, 0), (0, width - part.shape[1])))
        for part in (
            np.transpose(band_matrix(taps, cols, cols, HALF), (0, 2, 1)).reshape(3 * cols, cols),
            band_matrix(taps, rows, rows + 2 * TILE, HALF - TILE).reshape(3 * rows, -1),
            collect,
        )
    ]), BF16)
    hbm = pl.BlockSpec(memory_space=pltpu.HBM)
    vmem = pl.BlockSpec(memory_space=pltpu.VMEM)
    smem = pl.BlockSpec(memory_space=pltpu.SMEM)
    dma = pltpu.SemaphoreType.DMA
    cross = intersection.reshape(1, pieces)
    middle = pl.pallas_call(
        functools.partial(kernel, visits, strips, distinct),
        out_shape=(
            jax.ShapeDtypeStruct((rows, cols), BF16),
            jax.ShapeDtypeStruct((blocks, pieces, TILE, cols), BF16),
            jax.ShapeDtypeStruct((distinct, BASES * TILE, blocks * cols), BF16),
            jax.ShapeDtypeStruct((distinct, span, 2 * BASES * TILE), BF16),
        ),
        in_specs=[hbm, hbm, vmem, vmem, smem, smem, hbm],
        out_specs=(vmem, vmem, vmem, vmem),
        scratch_shapes=[
            pltpu.VMEM((blocks, pieces, TILE, cols), jnp.int32),
            pltpu.VMEM(tables.shape, BF16),
            pltpu.VMEM((span, blocks * cols), BF16),
            pltpu.VMEM((span, blocks * cols), BF16),
            pltpu.VMEM((blocks, distinct, 2, TILE, cols), BF16),
            pltpu.VMEM((visits, distinct, 2, TILE, cols), BF16),
            pltpu.VMEM((1, 128), F32),
            pltpu.VMEM((visits, 1, 128), F32),
            pltpu.VMEM((blocks + 2, visits, TILE, cols), BF16),
            pltpu.VMEM((distinct, len(pairs) * TILE, blocks * cols), BF16),
            pltpu.VMEM((BASES * 8, 128), F32),
            pltpu.VMEM((max(1, strips - 1), BASES * 8, 128), F32),
            dma((2, blocks)),
            dma,
            dma((blocks,)),
            dma((visits,)),
            dma((blocks,)),
            dma((visits,)),
            dma((visits,)),
            dma((blocks,)),
            dma((2,)),
            dma((2,)),
            dma((max(1, strips - 1),)),
            dma((max(1, strips - 1),)),
        ],
        compiler_params=pltpu.CompilerParams(
            collective_id=0, has_side_effects=True, vmem_limit_bytes=55_100_000
        ),
        name="coadd_solve",
    )(
        images, mask_bits, visit_weight, cross, patch_owner, cross,
        tables,
    )
    return pl.pallas_call(
        finish,
        out_shape=(
            jax.ShapeDtypeStruct((1, 1, rows, cols), BF16),
            jax.ShapeDtypeStruct(images.shape, BF16),
        ),
        in_specs=[vmem, vmem, vmem, vmem],
        out_specs=(hbm, hbm),
        scratch_shapes=[
            pltpu.VMEM((blocks, pieces, TILE, cols), BF16),
            dma((1 + blocks,)),
        ],
        compiler_params=pltpu.CompilerParams(vmem_limit_bytes=40 * 1024 * 1024),
        name="difference",
    )(*middle)


def solution(mesh):
    in_specs = (
        P("band", ("groups", "visit"), "strip", None),
        P("band", ("groups", "visit"), "strip", None),
        P("band", ("groups", "visit")),
        P(("groups", "visit"), None),
        P("groups"),
    )
    out_specs = (
        P("band", ("groups", "visit"), "strip", None),
        P("band", ("groups", "visit"), "strip", None),
    )
    step = functools.partial(body, mesh.shape["visit"], mesh.shape["strip"])
    return jax.shard_map(step, mesh=mesh, in_specs=in_specs, out_specs=out_specs, check_vma=False)
```
